32 devices in a mesh: groups: 2 (over x), dom: 16 (over z, y, core).
Axes of the slice: x: 2, y: 2, z: 4, core: 2. Of those that a mesh axis runs over, the one named last changes fastest.
Arguments:
- grid: bfloat16 [32768, 1024], P(('groups', 'dom')), parts along dimension 0, may hold values from -6 to 6
- latent_in: bfloat16 [512, 1024], P(('groups', 'dom')), parts along dimension 0, may hold values from -3 to 3
- grid_gain: float32 [1024], replicated, may hold values from 0.5 to 1.5
- node_gain: float32 [1024], replicated, may hold values from 0.5 to 1.5
- dec_gain: float32 [1024], replicated, may hold values from 0.5 to 1.5
- w_q_enc: bfloat16 [1024, 512], replicated
- w_kv_enc: bfloat16 [1024, 1024], replicated, may hold values from -0.1875 to 0.1875
- w_o_enc: bfloat16 [512, 1024], replicated, may hold values from -0.25 to 0.25
- w_q_dec: bfloat16 [1024, 512], replicated
- w_kv_dec: bfloat16 [1024, 1024], replicated, may hold values from -0.1875 to 0.1875
- w_o_dec: bfloat16 [512, 1024], replicated, may hold values from -0.25 to 0.25
- enc_need: int32 [16, 512], P('dom'), may hold values from 0 to 1023
- enc_slot: int32 [32, 256], P(None, 'dom'), may hold values from 0 to 511
- enc_count: int32 [256], P('dom'), may hold values from 1 to 32
- dec_need: int32 [16, 4096], P('dom'), may hold values from 0 to 15
- dec_slot: int32 [4, 16384], P(None, 'dom'), may hold values from 0 to 4095
Outputs:
- latent_out: bfloat16 [512, 1024], P(('groups', 'dom')), parts along dimension 0
- grid_out: bfloat16 [32768, 1024], P(('groups', 'dom')), parts along dimension 0
The draws below stay inside these ranges and needn't reach their ends.
There are 2 independent parts, one for each index of `groups`. The reference program is written for one: setup_inputs(seed, part) draws one part's arguments, and reference() takes and returns one part's arrays. A program takes and returns all parts, laid end to end along the dimension named above; an argument that names none is the same for every part. Nothing has to cross between parts.
Inputs may be any that keep to these rules, and one draw needn't show every extreme that they name: `enc_need`: a grid point's index within its band; entries may repeat. Edges of node n are enc_slot[0..enc_count[n]-1, n]; entries may repeat. `dec_need`: a latent node's index within its window; entries may repeat. `dec_slot`: entries may repeat.
All inputs are finite; a program needn't handle non-finite values.
Results may differ from the reference program's by a relative error of at most 0.02.
The reference program's roundings to bfloat16 on the way count: a program that leaves them out, or rounds other values in their place, can miss the bound.
Values may be sent and summed in bfloat16 or wider, within the bound.
A program may use at most 128 MiB of HBM per device.

```python
import math
import jax
import jax.numpy as jnp
from jax import lax

D = 1024
HEADS = 8
KE = 32
KD = 4
GP_DEV = 1024
NODE_DEV = 16
HH = 512
GRID = 16384
NODES = 256
N_DOM = 16


def query_weight(key):
    values = jax.random.normal(key, (D, HH), jnp.float32) * D ** (-0.5)
    values = values * 1.5
    return values.astype(jnp.bfloat16)


def draw_w_q_enc(key, part):
    return query_weight(jax.random.fold_in(key, 11))


def draw_w_q_dec(key, part):
    return query_weight(jax.random.fold_in(key, 23))


def with_ends(entries, own_key, smallest, largest):
    dims = entries.shape
    place = [jax.random.randint(jax.random.fold_in(own_key, axis), (), 0, dims[axis]) for axis in range(len(dims))]
    entries = entries.at[tuple(place)].set(smallest)
    longest = dims.index(max(dims))
    place[longest] = (place[longest] + 1) % dims[longest]
    return entries.at[tuple(place)].set(largest)


def levels(key, shape, cuts, least, top_value):
    factor_of, own = 1.0, jax.random.fold_in(key, 6)
    for dim, blocks in cuts:
        heights = jnp.exp(jax.random.uniform(jax.random.fold_in(own, dim), (blocks,), jnp.float32, least / len(cuts), top_value / len(cuts)))
        factor_of = factor_of * jnp.repeat(heights, shape[dim] // blocks).reshape([-1 if axis == dim else 1 for axis in range(len(shape))])
    return factor_of


def noise(own_key, shape, scale, reach, pieces=(), kind=jnp.bfloat16):
    array = scale * jax.random.normal(own_key, shape, jnp.float32)
    if pieces:
        array = array * levels(own_key, shape, pieces, -0.22, 0.18)
    return jnp.clip(array, -reach, reach).astype(kind)


def setup_inputs(seed: int = 0, part: int = 0) -> dict:
    keys = jax.random.split(jax.random.key(seed), 17)
    part_splits = jax.random.split(jax.random.fold_in(keys[16], part), 17)
    return {
        "grid": noise(part_splits[0], (GRID, D), 1.0, 6.0, ((0, 16),)),
        "latent_in": noise(part_splits[1], (NODES, D), 0.5, 3.0, ((0, 16),)),
        "grid_gain": jnp.clip(1.0 + 0.1 * jax.random.normal(keys[2], (D,), jnp.float32), 0.5, 1.5),
        "node_gain": jnp.clip(1.0 + 0.1 * jax.random.normal(keys[3], (D,), jnp.float32), 0.5, 1.5),
        "dec_gain": jnp.clip(1.0 + 0.1 * jax.random.normal(keys[4], (D,), jnp.float32), 0.5, 1.5),
        "w_q_enc": draw_w_q_enc(jax.random.fold_in(keys[16], 71), part),
        "w_kv_enc": noise(keys[6], (D, 2 * HH), D ** -0.5, 0.1875),
        "w_o_enc": noise(keys[7], (HH, D), HH ** -0.5, 0.25),
        "w_q_dec": draw_w_q_dec(jax.random.fold_in(keys[16], 71), part),
        "w_kv_dec": noise(keys[9], (D, 2 * HH), D ** -0.5, 0.1875),
        "w_o_dec": noise(keys[10], (HH, D), HH ** -0.5, 0.25),
        "enc_need": with_ends(jax.random.randint(keys[11], (N_DOM, NODE_DEV * KE), 0, GP_DEV), jax.random.fold_in(keys[11], 1), 0, GP_DEV - 1).astype(jnp.int32),
        "enc_slot": with_ends(jax.random.randint(keys[12], (KE, NODES), 0, NODE_DEV * KE), jax.random.fold_in(keys[12], 1), 0, (NODE_DEV * KE) - 1).astype(jnp.int32),
        "enc_count": with_ends(jax.random.randint(keys[13], (NODES,), 1, KE + 1), jax.random.fold_in(keys[13], 1), 1, KE).astype(jnp.int32),
        "dec_need": with_ends(jax.random.randint(keys[14], (N_DOM, GP_DEV * KD), 0, NODE_DEV), jax.random.fold_in(keys[14], 1), 0, NODE_DEV - 1).astype(jnp.int32),
        "dec_slot": with_ends(jax.random.randint(keys[15], (KD, GRID), 0, GP_DEV * KD), jax.random.fold_in(keys[15], 1), 0, (GP_DEV * KD) - 1).astype(jnp.int32),
    }


norm_eps = 1e-06

def rms_norm(values, weight_gain):
    widened = values.astype(jnp.float32)
    spread = lax.optimization_barrier(jnp.mean(widened * widened, axis=-1, keepdims=True))
    return (widened * lax.rsqrt(spread + norm_eps) * weight_gain).astype(jnp.bfloat16)

def attend_keys(queries, key_rows, keep_mask):
    rows_here = queries.shape[0]
    inner_width = queries.shape[1]
    head_size = inner_width // HEADS
    edge_count = key_rows.shape[0]
    query_heads = queries.reshape(rows_here, HEADS, head_size).astype(jnp.float32)
    key_heads = key_rows[..., :inner_width].reshape(edge_count, rows_here, HEADS, head_size).astype(jnp.float32)
    value_heads = key_rows[..., inner_width:].reshape(edge_count, rows_here, HEADS, head_size).astype(jnp.float32)
    scores = jnp.einsum('rhd,krhd->krh', query_heads, key_heads) * (1.0 / math.sqrt(head_size))
    if keep_mask is not None:
        scores = jnp.where(keep_mask[:, :, None], scores, -1e+30)
    highest = lax.optimization_barrier(jnp.max(scores, axis=0, keepdims=True))
    raised = jnp.exp(scores - highest)
    weights = (raised / lax.optimization_barrier(jnp.sum(raised, axis=0, keepdims=True))).astype(jnp.bfloat16)
    mixed = jnp.einsum('krh,krhd->rhd', weights.astype(jnp.float32), value_heads)
    return mixed.reshape(rows_here, inner_width).astype(jnp.bfloat16)

def reference(grid, latent_in, grid_gain, node_gain, dec_gain, w_q_enc, w_kv_enc, w_o_enc, w_q_dec, w_kv_dec, w_o_dec, enc_need, enc_slot, enc_count, dec_need, dec_slot):
    normed_grid = rms_norm(grid, grid_gain)
    grid_pairs = jnp.dot(normed_grid, w_kv_enc, preferred_element_type=jnp.float32).astype(jnp.bfloat16)
    enc_cap = NODE_DEV * KE // N_DOM
    enc_owner = jnp.arange(NODE_DEV * KE, dtype=jnp.int32) // enc_cap

    def encode_block(block):
        wanted = enc_owner * GP_DEV + enc_need[block]
        buffer = grid_pairs[wanted]
        start = (block * NODE_DEV).astype(jnp.int32)
        slots = lax.dynamic_slice_in_dim(enc_slot, start, NODE_DEV, 1)
        counts = lax.dynamic_slice_in_dim(enc_count, start, NODE_DEV, 0)
        own_rows = lax.dynamic_slice_in_dim(latent_in, start, NODE_DEV, 0)
        queries = jnp.dot(rms_norm(own_rows, node_gain), w_q_enc, preferred_element_type=jnp.float32).astype(jnp.bfloat16)
        keep_mask = jnp.arange(KE, dtype=jnp.int32)[:, None] < counts[None, :]
        mixed = attend_keys(queries, buffer[slots], keep_mask)
        update = jnp.dot(mixed, w_o_enc, preferred_element_type=jnp.float32)
        return (own_rows.astype(jnp.float32) + update).astype(jnp.bfloat16)
    latent_out = lax.map(encode_block, jnp.arange(N_DOM, dtype=jnp.int32)).reshape(NODES, D)
    latent_pairs = jnp.dot(rms_norm(latent_out, dec_gain), w_kv_dec, preferred_element_type=jnp.float32).astype(jnp.bfloat16)
    dec_cap = GP_DEV * KD // N_DOM
    dec_owner = jnp.arange(GP_DEV * KD, dtype=jnp.int32) // dec_cap

    def decode_block(block):
        wanted = dec_owner * NODE_DEV + dec_need[block]
        buffer = latent_pairs[wanted]
        start = (block * GP_DEV).astype(jnp.int32)
        slots = lax.dynamic_slice_in_dim(dec_slot, start, GP_DEV, 1)
        own_rows = lax.dynamic_slice_in_dim(grid, start, GP_DEV, 0)
        own_normed = lax.dynamic_slice_in_dim(normed_grid, start, GP_DEV, 0)
        queries = jnp.dot(own_normed, w_q_dec, preferred_element_type=jnp.float32).astype(jnp.bfloat16)
        mixed = attend_keys(queries, buffer[slots], None)
        update = jnp.dot(mixed, w_o_dec, preferred_element_type=jnp.float32)
        return (own_rows.astype(jnp.float32) + update).astype(jnp.bfloat16)
    grid_out = lax.map(decode_block, jnp.arange(N_DOM, dtype=jnp.int32)).reshape(GRID, D)
    return (latent_out, grid_out)
```

```python
import functools
import math

import jax
import jax.numpy as jnp
from jax import lax
from jax.experimental import pallas as pl
from jax.experimental.pallas import tpu as pltpu
from jax.sharding import PartitionSpec as P

HEADS = 8
norm_eps = 1e-06
F32 = jnp.float32
BF16 = jnp.bfloat16


def rms_norm(values, weight_gain):
    widened = values.astype(F32)
    spread = jnp.mean(widened * widened, axis=-1, keepdims=True)
    return (widened * lax.rsqrt(spread + norm_eps) * weight_gain).astype(BF16)


def attend_dense(queries, pairs, edges):
    rows, width = queries.shape
    head = width // HEADS
    q = queries.reshape(rows, HEADS, head)
    k = pairs[:, :width].reshape(-1, HEADS, head)
    v = pairs[:, width:].reshape(-1, HEADS, head)
    scores = jnp.einsum("rhd,khd->hrk", q, k, preferred_element_type=F32)
    scores = jnp.where(edges[None] > 0, scores * (1.0 / math.sqrt(head)), -1e30)
    highest = jnp.max(scores, axis=-1, keepdims=True)
    raised = jnp.exp(scores - highest) * edges[None]
    weights = (raised / jnp.sum(raised, axis=-1, keepdims=True)).astype(BF16)
    mixed = jnp.einsum("hrk,khd->rhd", weights, v, preferred_element_type=F32)
    return mixed.reshape(rows, width).astype(BF16)


def on_device(grid, latent_in, grid_gain, node_gain, dec_gain, w_q_enc, w_kv_enc, w_o_enc,
              w_q_dec, w_kv_dec, w_o_dec, enc_need, enc_slot, enc_count, dec_need, dec_slot):
    peers = lax.axis_size("dom")
    nodes = latent_in.shape[0]
    normed_grid = rms_norm(grid, grid_gain)
    wanted = lax.all_to_all(enc_need.reshape(peers, -1), "dom", split_axis=0, concat_axis=0, tiled=True)
    band = jnp.arange(grid.shape[0], dtype=jnp.int32)
    pick = (wanted.reshape(-1)[:, None] == band[None, :]).astype(BF16)
    chosen = jnp.dot(pick, normed_grid, preferred_element_type=F32).astype(BF16)
    rows = jnp.dot(chosen, w_kv_enc, preferred_element_type=F32).astype(BF16)
    arrived = lax.all_to_all(rows, "dom", split_axis=0, concat_axis=0, tiled=True)
    enc_queries = jnp.dot(rms_norm(latent_in, node_gain), w_q_enc, preferred_element_type=F32).astype(BF16)
    live = jnp.arange(enc_slot.shape[0], dtype=jnp.int32)[:, None] < enc_count[None, :]
    slot_row = jnp.arange(enc_need.shape[1], dtype=jnp.int32)
    enc_edges = jnp.sum((live[:, :, None] & (enc_slot[:, :, None] == slot_row)).astype(F32), axis=0)
    enc_mixed = attend_dense(enc_queries, arrived, enc_edges)
    enc_update = jnp.dot(enc_mixed, w_o_enc, preferred_element_type=F32)
    latent_out = (latent_in.astype(F32) + enc_update).astype(BF16)
    latent_pairs = jnp.dot(rms_norm(latent_out, dec_gain), w_kv_dec, preferred_element_type=F32).astype(BF16)
    dec_queries = jnp.dot(normed_grid, w_q_dec, preferred_element_type=F32).astype(BF16)
    everyone = lax.all_gather(latent_pairs, "dom", axis=0, tiled=True)
    total = dec_need.shape[1]
    cap = total // peers
    lanes = 128
    table = dec_need.reshape(total // lanes, lanes).astype(BF16)
    high = (dec_slot // lanes)[:, :, None] == jnp.arange(total // lanes, dtype=jnp.int32)
    low = (dec_slot % lanes)[:, :, None] == jnp.arange(lanes, dtype=jnp.int32)
    need = jnp.einsum("jgt,tl->jgl", high.astype(BF16), table, preferred_element_type=F32)
    need = jnp.sum(jnp.where(low, need, 0.0), axis=-1).astype(jnp.int32)
    node = (dec_slot // cap) * nodes + need
    dec_edges = jnp.sum((node[:, :, None] == jnp.arange(peers * nodes, dtype=jnp.int32)).astype(F32), axis=0)
    dec_mixed = attend_dense(dec_queries, everyone, dec_edges)
    dec_update = jnp.dot(dec_mixed, w_o_dec, preferred_element_type=F32)
    grid_out = (grid.astype(F32) + dec_update).astype(BF16)
    return (latent_out, grid_out)


NT = (((1,), (1,)), ((), ()))
TN = (((0,), (0,)), ((), ()))
HIGH = lax.Precision.HIGHEST


def iota(shape, dim):
    return lax.broadcasted_iota(jnp.int32, shape, dim)


def norm_into(values, gain):
    widened = values.astype(F32)
    spread = jnp.mean(widened * widened, axis=-1, keepdims=True)
    return (widened * lax.rsqrt(spread + norm_eps) * gain).astype(BF16)


def encoder_kernel(
    peers, grid_hbm, latent_hbm, ggain_hbm, ngain_hbm, dgain_hbm, wq_hbm, wkv_hbm, wo_hbm, wqd_hbm, wkvd_hbm,
    need_hbm, slot_hbm, count_hbm, dslot_hbm, table_hbm,
    latent_hbm_out, pairs_hbm, queries_hbm, bias_hbm,
    grid_v, latent_v, ggain_v, ngain_v, dgain_v, wq_v, wkv_v, wo_v, wqd_v, wkvd_v, need_v, slot_v, count_v, dslot_v,
    table_v, normed, chosen, rows, fan_of, query_mine, edges_mine,
    need_all, query_all, edges_all, mix_send, stat_send, mix_all, stat_all, pairs_all,
    latent_new, queries_out, bias_out, node_of, worth_of, load_sem, store_sem, send_sem, recv_sem, push_send, push_recv,
):
    me = lax.axis_index("dom")
    nodes, model = latent_v.shape
    width = wq_v.shape[1]
    head = width // HEADS
    cap = need_v.shape[1] // peers
    group = 128 // cap
    chips = peers // 2
    side = lax.rem(me, 2)
    partner = me + 1 - 2 * side
    points = grid_v.shape[0]
    lanes = HEADS * nodes
    both = 2 * cap
    blocks = push_send.shape[0]
    block = points // blocks

    barrier = pltpu.get_barrier_semaphore()
    for to in [lax.rem(me + 2 * step, peers) for step in range(1, chips)] + [partner]:
        pl.semaphore_signal(barrier, inc=1, device_id={"dom": to}, device_id_type=pl.DeviceIdType.MESH)

    def block_at(number):
        return slice(number * block, (number + 1) * block)

    pairs_of_refs = {
        "slot": (slot_hbm, slot_v), "count": (count_hbm, count_v), "need": (need_hbm, need_v),
        "latent": (latent_hbm, latent_v), "ngain": (ngain_hbm, ngain_v), "wq": (wq_hbm, wq_v),
        "ggain": (ggain_hbm, ggain_v),
    }
    for number in range(blocks):
        pairs_of_refs[number] = (grid_hbm.at[block_at(number)], grid_v.at[block_at(number)])
    pairs_of_refs.update({
        "wkv": (wkv_hbm, wkv_v), "wqd": (wqd_hbm, wqd_v), "dslot": (dslot_hbm, dslot_v), "table": (table_hbm, table_v),
        "wo": (wo_hbm, wo_v), "dgain": (dgain_hbm, dgain_v), "wkvd": (wkvd_hbm, wkvd_v),
    })
    loads = {}
    for number, (name, (source, target)) in enumerate(pairs_of_refs.items()):
        loads[name] = pltpu.make_async_copy(source, target, load_sem.at[number])
        loads[name].start()

    def message(kind, source, target, to, leaving, landing):
        return pltpu.make_async_remote_copy(
            src_ref=source,
            dst_ref=target,
            send_sem=send_sem.at[kind, leaving],
            recv_sem=recv_sem.at[kind, landing],
            device_id={"dom": to},
            device_id_type=pl.DeviceIdType.MESH,
        )

    def chip(step):
        return lax.rem(me + 2 * step, peers)

    def need_to(step, slot):
        return message(0, need_v, need_all.at[slot], chip(step), step, slot)

    def edges_to(step, slot):
        return message(1, edges_mine.at[chip(step) // group], edges_all.at[slot], chip(step), step, slot)

    def query_to(step, slot):
        return message(2, query_mine, query_all.at[slot], chip(step), step, slot)

    def mix_to(step, slot):
        return message(3, mix_send.at[step], mix_all.at[slot], chip(step), step, slot)

    def stat_to(step, slot):
        return message(4, stat_send.at[step], stat_all.at[slot], chip(step), step, slot)

    def pairs_to(step, slot):
        return message(5, pairs_all.at[me], pairs_all.at[me], chip(step), step, slot)

    def pairs_on(step, slot):
        owner = chip(step)
        return message(6, pairs_all.at[owner], pairs_all.at[owner], partner, step, slot)

    def push(number):
        return pltpu.make_async_remote_copy(
            src_ref=normed.at[0, block_at(number)],
            dst_ref=normed.at[1, block_at(number)],
            send_sem=push_send.at[number],
            recv_sem=push_recv.at[number],
            device_id={"dom": partner},
            device_id_type=pl.DeviceIdType.MESH,
        )

    others = range(1, chips)

    loads["slot"].wait()
    loads["count"].wait()
    edge_total = slot_v.shape[1]
    own = iota((nodes, nodes), 0) == iota((nodes, nodes), 1)
    counts = jnp.sum(jnp.where(own, count_v[...].astype(F32), 0.0), axis=1, keepdims=True)
    slots = jnp.where(iota(slot_v.shape, 1).astype(F32) < counts, slot_v[...], -1)
    entry = iota((nodes, peers * cap), 1)
    tally = jnp.zeros((nodes, peers * cap), F32)
    for j in range(edge_total):
        tally = tally + jnp.where(slots[:, j : j + 1] == entry, 1.0, 0.0)
    tally = tally.astype(BF16)
    for part in range(peers // group):
        edges_mine[part] = tally[:, part * 128 : (part + 1) * 128]
    edges_all[0] = edges_mine[me // group]
    fan_row = iota((chips * nodes, chips * lanes), 0)
    fan_lane = iota((chips * nodes, chips * lanes), 1)
    fan = fan_row == (fan_lane // lanes) * nodes + lax.rem(fan_lane, nodes)
    fan_of[...] = jnp.where(fan, 1.0, 0.0).astype(BF16)
    loads["need"].wait()
    need_all[0] = need_v[...]
    loads["latent"].wait()
    loads["ngain"].wait()
    loads["wq"].wait()
    queries = jnp.dot(
        norm_into(latent_v[...], ngain_v[...]), wq_v[...], preferred_element_type=F32
    ).astype(BF16)
    query_mine[...] = queries
    query_all[0] = queries

    pl.semaphore_wait(barrier, chips)
    for step in others:
        need_to(step, chips - step).start()
    for step in others:
        edges_to(step, chips - step).start()
        query_to(step, chips - step).start()

    loads["ggain"].wait()
    for number in range(blocks):
        loads[number].wait()

        def norm_block(piece, carry):
            at = pl.ds(pl.multiple_of(number * block + piece * 128, 128), 128)
            normed[0, at, :] = norm_into(grid_v[at, :], ggain_v[...])
            return carry

        lax.fori_loop(0, block // 128, norm_block, 0)
        push(number).start()

    for step in others:
        need_to(step, step).wait_recv()
    base = pl.multiple_of((me // group) * 128, 128)
    lists = need_all[:, :, pl.ds(base, 128)]
    within = lax.rem(me // 2, group // 2) * both
    asked = jnp.broadcast_to(lists, (chips, cap, 128)).astype(F32)
    spot = iota((chips, cap, 128), 1)
    lane = iota((chips, cap, 128), 2)
    wanted = []
    for band in (side, 1 - side):
        picked = jnp.where(lane == within + band * cap + spot, asked, 0.0)
        wanted.append(jnp.sum(picked, axis=2, keepdims=True).astype(jnp.int32).reshape(chips * cap, 1))
    point = iota((chips * cap, points), 1)
    pick = jnp.where(wanted[0] == point, 1.0, 0.0).astype(BF16)
    chosen[: chips * cap] = jnp.dot(pick, normed[0], preferred_element_type=F32).astype(BF16)
    pick = jnp.where(wanted[1] == point, 1.0, 0.0).astype(BF16)
    for number in range(blocks):
        push(number).wait_recv()
    chosen[chips * cap :] = jnp.dot(pick, normed[1], preferred_element_type=F32).astype(BF16)
    loads["wkv"].wait()
    rows[...] = jnp.dot(chosen[...], wkv_v[...], preferred_element_type=F32).astype(BF16)

    for step in others:
        edges_to(step, step).wait_recv()
    spot = iota((both, 128), 0)
    band = jnp.where(spot < cap, side, 1 - side)
    mine = iota((both, 128), 1) == within + band * cap + lax.rem(spot, cap)
    entries = lax.dot_general(
        jnp.where(mine, 1.0, 0.0).astype(BF16), edges_all[...].reshape(chips * nodes, 128), NT,
        preferred_element_type=F32,
    ).astype(BF16)
    entries = jnp.dot(entries, fan_of[...], preferred_element_type=F32)
    for step in others:
        query_to(step, step).wait_recv()

    own_head = iota((lanes, width), 0) // nodes == iota((lanes, width), 1) // head

    def window(w):
        spread_query = jnp.broadcast_to(query_all[w][None], (HEADS, nodes, width)).reshape(lanes, width)
        spread_query = jnp.where(own_head, spread_query, jnp.zeros_like(spread_query))
        near = slice(w * cap, (w + 1) * cap)
        far = slice((chips + w) * cap, (chips + w + 1) * cap)
        keys_here = jnp.concatenate([rows[near, :width], rows[far, :width]], axis=0)
        values_here = jnp.concatenate([rows[near, width:], rows[far, width:]], axis=0)
        scores = lax.dot_general(keys_here, spread_query, NT, preferred_element_type=F32)
        times = entries[:, w * lanes : (w + 1) * lanes]
        scores = jnp.where(times > 0, scores * (1.0 / math.sqrt(head)), -1e30)
        highest = jnp.max(scores, axis=0, keepdims=True)
        raised = jnp.exp(scores - highest) * times
        total = jnp.sum(raised, axis=0, keepdims=True)
        mixed = lax.dot_general(raised.astype(BF16), values_here, TN, preferred_element_type=F32)
        mixed = jnp.where(own_head, mixed, 0.0).reshape(HEADS, nodes, width)
        return jnp.sum(mixed, axis=0).astype(BF16), highest, total

    for step, answer in [(step, window(step)) for step in range(chips)]:
        mixes, stats = (mix_all, stat_all) if step == 0 else (mix_send, stat_send)
        mixes[step] = answer[0]
        stats[step, 0:1, :] = answer[1]
        stats[step, 1:2, :] = answer[2]
    for step in others:
        mix_to(step, chips - step).start()
        stat_to(step, chips - step).start()

    loads["wqd"].wait()
    scale = math.log2(math.e) / math.sqrt(head)
    queries_out[...] = (jnp.dot(normed[0], wqd_v[...], preferred_element_type=F32) * scale).astype(BF16)
    queries_store = pltpu.make_async_copy(queries_out, queries_hbm, store_sem.at[0])
    queries_store.start()

    loads["dslot"].wait()
    loads["table"].wait()
    keys = peers * nodes
    dec_cap = table_v.shape[0] * 128 // peers
    slots = dslot_v[...]
    edge_total = slots.shape[0]
    slots = jnp.concatenate([slots] * (8 // edge_total), axis=0)
    columns = []
    for part in range(points // 128):
        piece = slots[:, part * 128 : (part + 1) * 128]
        high = piece // 128
        low = lax.rem(piece, 128)
        need = jnp.zeros_like(piece)
        for line in range(table_v.shape[0]):
            entry = jnp.broadcast_to(table_v[line : line + 1, :], piece.shape)
            need = jnp.where(high == line, jnp.take_along_axis(entry, low, axis=1), need)
        columns.append((piece // dec_cap) * nodes + need)
    node = jnp.concatenate(columns, axis=1)
    times = jnp.ones(node.shape, F32)
    for j in range(1, edge_total):
        times = times + jnp.where(node == jnp.concatenate([node[j:], node[:j]], axis=0), 1.0, 0.0)
    node_of[...] = node.astype(F32).T
    worth_of[...] = jnp.log2(times).T
    name = iota((128, keys), 1).astype(F32)

    def bias_block(piece, carry):
        at = pl.ds(pl.multiple_of(piece * 128, 128), 128)
        nodes_here, worth_here = node_of[at, :], worth_of[at, :]
        bias = jnp.full((128, keys), -1e30, F32)
        for j in range(edge_total):
            bias = jnp.where(nodes_here[:, j : j + 1] == name, worth_here[:, j : j + 1], bias)
        bias_out[at, :] = bias
        return carry

    lax.fori_loop(0, points // 128, bias_block, 0)
    bias_store = pltpu.make_async_copy(bias_out, bias_hbm, store_sem.at[1])
    bias_store.start()
    loads["wo"].wait()
    loads["dgain"].wait()
    loads["wkvd"].wait()

    for step in others:
        stat_to(step, step).wait_recv()
    tops = [stat_all[step, 0:1, :] for step in range(chips)]
    sums = [stat_all[step, 1:2, :] for step in range(chips)]
    top = functools.reduce(jnp.maximum, tops)
    shares = [jnp.exp(one - top) for one in tops]
    whole = functools.reduce(jnp.add, [a * b for a, b in zip(shares, sums)])
    own_node = iota((nodes, lanes), 0) == lax.rem(iota((nodes, lanes), 1), nodes)
    stacked = jnp.concatenate([jnp.where(own_node, share / whole, 0.0) for share in shares], axis=0)
    widen = (iota((lanes, width), 0) // nodes == iota((lanes, width), 1) // head).astype(F32)
    factors = jnp.dot(stacked, widen, precision=HIGH, preferred_element_type=F32).reshape(chips, nodes, width)
    for step in others:
        mix_to(step, step).wait_recv()
    enc_mixed = jnp.sum(factors * mix_all[...].astype(F32), axis=0).astype(BF16)
    update = jnp.dot(enc_mixed, wo_v[...], preferred_element_type=F32)
    fresh = (latent_v[...].astype(F32) + update).astype(BF16)
    latent_new[...] = fresh
    latent_store = pltpu.make_async_copy(latent_new, latent_hbm_out, store_sem.at[2])
    latent_store.start()
    pairs = jnp.dot(norm_into(fresh, dgain_v[...]), wkvd_v[...], preferred_element_type=F32).astype(BF16)
    pairs_all[me] = pairs
    for step in others:
        pairs_to(step, chips - step).start()
    pairs_near = message(6, pairs_all.at[me], pairs_all.at[me], partner, 0, 0)
    pairs_near.start()

    for step in others:
        pairs_to(step, step).wait_recv()
        pairs_on(step, step).start()
    pairs_near.wait_recv()
    for step in others:
        pairs_on(step, step).wait_recv()
    pairs_store = pltpu.make_async_copy(pairs_all, pairs_hbm, store_sem.at[3])
    pairs_store.start()

    for step in others:
        for outgoing in (need_to, edges_to, query_to, mix_to, stat_to, pairs_to, pairs_on):
            outgoing(step, step).wait_send()
    pairs_near.wait_send()
    for number in range(blocks):
        push(number).wait_send()
    queries_store.wait()
    bias_store.wait()
    latent_store.wait()
    pairs_store.wait()


BLOCKS = 4


def encode(grid, latent_in, grid_gain, node_gain, dec_gain, w_q_enc, w_kv_enc, w_o_enc, w_q_dec, w_kv_dec,
           enc_need, enc_slot, enc_count, dec_slot, dec_need):
    peers = lax.axis_size("dom")
    nodes, model = latent_in.shape
    width = w_q_enc.shape[1]
    entries = enc_need.shape[1]
    cap = entries // peers
    points = grid.shape[0]
    chips = peers // 2
    lanes = HEADS * nodes
    far = pl.BlockSpec(memory_space=pl.ANY)
    operands = (grid, latent_in, grid_gain[None], node_gain[None], dec_gain[None], w_q_enc, w_kv_enc, w_o_enc, w_q_dec,
                w_kv_dec, enc_need, enc_slot.T, enc_count[None], dec_slot, dec_need.reshape(-1, 128))
    latent_out, pairs, queries, bias = pl.pallas_call(
        functools.partial(encoder_kernel, peers),
        name="encode",
        out_shape=(
            jax.ShapeDtypeStruct((nodes, model), BF16),
            jax.ShapeDtypeStruct((peers, nodes, 2 * width), BF16),
            jax.ShapeDtypeStruct((points, width), BF16),
            jax.ShapeDtypeStruct((points, peers * nodes), F32),
        ),
        in_specs=[far] * len(operands),
        out_specs=(far,) * 4,
        scratch_shapes=[pltpu.VMEM(one.shape, one.dtype) for one in operands] + [
            pltpu.VMEM((2, points, model), BF16),
            pltpu.VMEM((entries, model), BF16),
            pltpu.VMEM((entries, 2 * width), BF16),
            pltpu.VMEM((chips * nodes, chips * lanes), BF16),
            pltpu.VMEM((nodes, width), BF16),
            pltpu.VMEM((entries // 128, nodes, 128), BF16),
            pltpu.VMEM((chips, 1, entries), jnp.int32),
            pltpu.VMEM((chips, nodes, width), BF16),
            pltpu.VMEM((chips, nodes, 128), BF16),
            pltpu.VMEM((chips, nodes, width), BF16),
            pltpu.VMEM((chips, 2, lanes), F32),
            pltpu.VMEM((chips, nodes, width), BF16),
            pltpu.VMEM((chips, 2, lanes), F32),
            pltpu.VMEM((peers, nodes, 2 * width), BF16),
            pltpu.VMEM((nodes, model), BF16),
            pltpu.VMEM((points, width), BF16),
            pltpu.VMEM((points, peers * nodes), F32),
            pltpu.VMEM((points, 8), F32),
            pltpu.VMEM((points, 8), F32),
            pltpu.SemaphoreType.DMA((len(operands) - 1 + BLOCKS,)),
            pltpu.SemaphoreType.DMA((4,)),
            pltpu.SemaphoreType.DMA((7, chips)),
            pltpu.SemaphoreType.DMA((7, chips)),
            pltpu.SemaphoreType.DMA((BLOCKS,)),
            pltpu.SemaphoreType.DMA((BLOCKS,)),
        ],
        compiler_params=pltpu.CompilerParams(
            collective_id=0, has_side_effects=True, vmem_limit_bytes=60 * 1024 * 1024
        ),
    )(*operands)
    return latent_out, pairs.reshape(peers * nodes, 2 * width), queries, bias


def decoder_kernel(query_hbm, pairs_hbm, bias_hbm, grid_hbm, wo_hbm, latent_ref, out_hbm, latent_out,
                   query_v, pairs_v, bias_v, grid_v, wo_v, out_v, keys_of, values_of, mixed, load_sem, store_sem):
    points, width = query_v.shape
    head = width // HEADS
    keys = pairs_v.shape[0]
    quad = 4
    chunks = CHUNKS
    tile = points // chunks

    def rows(part):
        return slice(part * tile, (part + 1) * tile)

    load_pairs = pltpu.make_async_copy(pairs_hbm, pairs_v, load_sem.at[0])
    load_wo = pltpu.make_async_copy(wo_hbm, wo_v, load_sem.at[1])
    load_query = [
        pltpu.make_async_copy(query_hbm.at[rows(part)], query_v.at[rows(part)], load_sem.at[2 + part])
        for part in range(chunks)
    ]
    load_bias = [
        pltpu.make_async_copy(bias_hbm.at[rows(part)], bias_v.at[rows(part)], load_sem.at[2 + chunks + part])
        for part in range(chunks)
    ]
    load_grid = pltpu.make_async_copy(grid_hbm, grid_v, load_sem.at[2 + 2 * chunks])
    load_pairs.start()
    for part in range(chunks):
        load_query[part].start()
        load_bias[part].start()
    load_wo.start()
    load_grid.start()

    latent_out[...] = latent_ref[...]
    load_pairs.wait()
    lane_head = iota((keys, quad * head), 1) // head
    for h in range(HEADS):
        some = pairs_v[:, (h // quad) * quad * head : (h // quad + 1) * quad * head]
        keys_of[h] = jnp.where(lane_head == h % quad, some, jnp.zeros_like(some))
    side_of = iota((keys, 2 * head), 1) // head
    for pair in range(HEADS // 2):
        some = pairs_v[:, width + pair * 2 * head : width + (pair + 1) * 2 * head]
        for side in range(2):
            own = side_of == side
            at = slice(side * keys, (side + 1) * keys)
            values_of[pair, at, : 2 * head] = jnp.where(own, some, jnp.zeros_like(some))
            values_of[pair, at, 2 * head :] = jnp.where(own, jnp.ones_like(some), jnp.zeros_like(some))

    stores = []
    for part in range(chunks):
        at = rows(part)
        load_query[part].wait()
        load_bias[part].wait()
        for pair in range(HEADS // 2):
            four = 2 * pair // quad
            query = query_v[at, four * quad * head : (four + 1) * quad * head]
            raised = []
            for side in range(2):
                scores = lax.dot_general(query, keys_of[2 * pair + side], NT, preferred_element_type=F32)
                scores = scores + bias_v[at, :]
                highest = jnp.max(scores, axis=1, keepdims=True)
                raised.append(jnp.exp2(scores - highest).astype(BF16))
            got = jnp.dot(jnp.concatenate(raised, axis=1), values_of[pair], preferred_element_type=F32)
            mixed[at, pair * 2 * head : (pair + 1) * 2 * head] = (got[:, : 2 * head] / got[:, 2 * head :]).astype(BF16)
        if part == 0:
            load_wo.wait()
            load_grid.wait()
        update = jnp.dot(mixed[at, :], wo_v[...], preferred_element_type=F32)
        out_v[at, :] = (grid_v[at, :].astype(F32) + update).astype(BF16)
        stores.append(pltpu.make_async_copy(out_v.at[at], out_hbm.at[at], store_sem.at[part]))
        stores[-1].start()
    for store in stores:
        store.wait()


CHUNKS = 2


def decode(queries, pairs, bias, grid, w_o_dec, latent_out):
    points, model = grid.shape
    width = queries.shape[1]
    keys = pairs.shape[0]
    vmem = pl.BlockSpec(memory_space=pltpu.VMEM)
    far = pl.BlockSpec(memory_space=pl.ANY)
    return pl.pallas_call(
        decoder_kernel,
        name="decode",
        out_shape=(
            jax.ShapeDtypeStruct(grid.shape, BF16),
            jax.ShapeDtypeStruct(latent_out.shape, BF16),
        ),
        in_specs=[far, far, far, far, far, vmem],
        out_specs=(far, vmem),
        scratch_shapes=[
            pltpu.VMEM(queries.shape, BF16),
            pltpu.VMEM(pairs.shape, BF16),
            pltpu.VMEM(bias.shape, F32),
            pltpu.VMEM(grid.shape, BF16),
            pltpu.VMEM(w_o_dec.shape, BF16),
            pltpu.VMEM(grid.shape, BF16),
            pltpu.VMEM((HEADS, keys, width // 2), BF16),
            pltpu.VMEM((HEADS // 2, 2 * keys, 4 * width // HEADS), BF16),
            pltpu.VMEM((points, width), BF16),
            pltpu.SemaphoreType.DMA((3 + 2 * CHUNKS,)),
            pltpu.SemaphoreType.DMA((CHUNKS,)),
        ],
    )(queries, pairs, bias, grid, w_o_dec, latent_out)


def by_kernels(grid, latent_in, grid_gain, node_gain, dec_gain, w_q_enc, w_kv_enc, w_o_enc,
               w_q_dec, w_kv_dec, w_o_dec, enc_need, enc_slot, enc_count, dec_need, dec_slot):
    latent_out, pairs, queries, bias = encode(
        grid, latent_in, grid_gain, node_gain, dec_gain, w_q_enc, w_kv_enc, w_o_enc, w_q_dec, w_kv_dec,
        enc_need, enc_slot, enc_count, dec_slot, dec_need)
    grid_out, latent_out = decode(queries, pairs, bias, grid, w_o_dec, latent_out)
    return (latent_out, grid_out)


def chosen_form(*args):
    grid, latent_in, enc_need, dec_slot = args[0], args[1], args[11], args[15]
    peers = lax.axis_size("dom")
    cap = enc_need.shape[1] // peers
    small = latent_in.shape[0] * peers <= 256
    fits = peers % 2 == 0 and 128 % cap == 0 and cap in (32, 64) and HEADS * latent_in.shape[0] == 128 and grid.shape[0] % 512 == 0
    if small and fits and 8 % dec_slot.shape[0] == 0:
        return by_kernels(*args)
    return on_device(*args)


def solution(mesh):
    both, rep = P(("groups", "dom"), None), P()
    return jax.shard_map(
        chosen_form,
        mesh=mesh,
        in_specs=(both, both, *([rep] * 9), P("dom", None), P(None, "dom"), P("dom"), P("dom", None), P(None, "dom")),
        out_specs=(both, both),
        check_vma=False,
    )
```

```python
import functools
import math

import jax
import jax.numpy as jnp
from jax import lax
from jax.experimental import pallas as pl
from jax.experimental.pallas import tpu as pltpu
from jax.sharding import PartitionSpec as P

HEADS = 8
norm_eps = 1e-06
F32 = jnp.float32
BF16 = jnp.bfloat16


def rms_norm(values, weight_gain):
    widened = values.astype(F32)
    spread = jnp.mean(widened * widened, axis=-1, keepdims=True)
    return (widened * lax.rsqrt(spread + norm_eps) * weight_gain).astype(BF16)


def attend_dense(queries, pairs, edges):
    rows, width = queries.shape
    head = width // HEADS
    q = queries.reshape(rows, HEADS, head)
    k = pairs[:, :width].reshape(-1, HEADS, head)
    v = pairs[:, width:].reshape(-1, HEADS, head)
    scores = jnp.einsum("rhd,khd->hrk", q, k, preferred_element_type=F32)
    scores = jnp.where(edges[None] > 0, scores * (1.0 / math.sqrt(head)), -1e30)
    highest = jnp.max(scores, axis=-1, keepdims=True)
    raised = jnp.exp(scores - highest) * edges[None]
    weights = (raised / jnp.sum(raised, axis=-1, keepdims=True)).astype(BF16)
    mixed = jnp.einsum("hrk,khd->rhd", weights, v, preferred_element_type=F32)
    return mixed.reshape(rows, width).astype(BF16)


def on_device(grid, latent_in, grid_gain, node_gain, dec_gain, w_q_enc, w_kv_enc, w_o_enc,
              w_q_dec, w_kv_dec, w_o_dec, enc_need, enc_slot, enc_count, dec_need, dec_slot):
    peers = lax.axis_size("dom")
    nodes = latent_in.shape[0]
    normed_grid = rms_norm(grid, grid_gain)
    wanted = lax.all_to_all(enc_need.reshape(peers, -1), "dom", split_axis=0, concat_axis=0, tiled=True)
    band = jnp.arange(grid.shape[0], dtype=jnp.int32)
    pick = (wanted.reshape(-1)[:, None] == band[None, :]).astype(BF16)
    chosen = jnp.dot(pick, normed_grid, preferred_element_type=F32).astype(BF16)
    rows = jnp.dot(chosen, w_kv_enc, preferred_element_type=F32).astype(BF16)
    arrived = lax.all_to_all(rows, "dom", split_axis=0, concat_axis=0, tiled=True)
    enc_queries = jnp.dot(rms_norm(latent_in, node_gain), w_q_enc, preferred_element_type=F32).astype(BF16)
    live = jnp.arange(enc_slot.shape[0], dtype=jnp.int32)[:, None] < enc_count[None, :]
    slot_row = jnp.arange(enc_need.shape[1], dtype=jnp.int32)
    enc_edges = jnp.sum((live[:, :, None] & (enc_slot[:, :, None] == slot_row)).astype(F32), axis=0)
    enc_mixed = attend_dense(enc_queries, arrived, enc_edges)
    enc_update = jnp.dot(enc_mixed, w_o_enc, preferred_element_type=F32)
    latent_out = (latent_in.astype(F32) + enc_update).astype(BF16)
    latent_pairs = jnp.dot(rms_norm(latent_out, dec_gain), w_kv_dec, preferred_element_type=F32).astype(BF16)
    dec_queries = jnp.dot(normed_grid, w_q_dec, preferred_element_type=F32).astype(BF16)
    everyone = lax.all_gather(latent_pairs, "dom", axis=0, tiled=True)
    total = dec_need.shape[1]
    cap = total // peers
    lanes = 128
    table = dec_need.reshape(total // lanes, lanes).astype(BF16)
    high = (dec_slot // lanes)[:, :, None] == jnp.arange(total // lanes, dtype=jnp.int32)
    low = (dec_slot % lanes)[:, :, None] == jnp.arange(lanes, dtype=jnp.int32)
    need = jnp.einsum("jgt,tl->jgl", high.astype(BF16), table, preferred_element_type=F32)
    need = jnp.sum(jnp.where(low, need, 0.0), axis=-1).astype(jnp.int32)
    node = (dec_slot // cap) * nodes + need
    dec_edges = jnp.sum((node[:, :, None] == jnp.arange(peers * nodes, dtype=jnp.int32)).astype(F32), axis=0)
    dec_mixed = attend_dense(dec_queries, everyone, dec_edges)
    dec_update = jnp.dot(dec_mixed, w_o_dec, preferred_element_type=F32)
    grid_out = (grid.astype(F32) + dec_update).astype(BF16)
    return (latent_out, grid_out)


NT = (((1,), (1,)), ((), ()))
TN = (((0,), (0,)), ((), ()))
HIGH = lax.Precision.HIGHEST


def iota(shape, dim):
    return lax.broadcasted_iota(jnp.int32, shape, dim)


def norm_into(values, gain):
    widened = values.astype(F32)
    spread = jnp.mean(widened * widened, axis=-1, keepdims=True)
    return (widened * lax.rsqrt(spread + norm_eps) * gain).astype(BF16)


def encoder_kernel(
    peers, grid_hbm, latent_hbm, ggain_hbm, ngain_hbm, dgain_hbm, wq_hbm, wkv_hbm, wo_hbm, wqd_hbm, wkvd_hbm,
    need_hbm, slot_hbm, count_hbm, dslot_hbm, table_hbm, wod_hbm,
    latent_new, pairs_out, queries_out, bias_out, grid_v, wod_v,
    latent_v, ggain_v, ngain_v, dgain_v, wq_v, wkv_v, wo_v, wqd_v, wkvd_v, need_v, slot_v, count_v, dslot_v,
    table_v, normed, chosen, rows, fan_of, query_mine, edges_mine,
    need_all, query_all, edges_all, mix_send, stat_send, mix_all, stat_all, pairs_all,
    node_of, worth_of, load_sem, send_sem, recv_sem, push_send, push_recv,
):
    me = lax.axis_index("dom")
    nodes, model = latent_v.shape
    width = wq_v.shape[1]
    head = width // HEADS
    cap = need_v.shape[1] // peers
    group = 128 // cap
    chips = peers // 2
    side = lax.rem(me, 2)
    partner = me + 1 - 2 * side
    points = grid_v.shape[0]
    lanes = HEADS * nodes
    both = 2 * cap
    blocks = push_send.shape[0]
    block = points // blocks

    barrier = pltpu.get_barrier_semaphore()
    for to in [lax.rem(me + 2 * step, peers) for step in range(1, chips)] + [partner]:
        pl.semaphore_signal(barrier, inc=1, device_id={"dom": to}, device_id_type=pl.DeviceIdType.MESH)

    def block_at(number):
        return slice(number * block, (number + 1) * block)

    pairs_of_refs = {
        "slot": (slot_hbm, slot_v), "count": (count_hbm, count_v), "need": (need_hbm, need_v),
        "latent": (latent_hbm, latent_v), "ngain": (ngain_hbm, ngain_v), "wq": (wq_hbm, wq_v),
        "ggain": (ggain_hbm, ggain_v),
    }
    for number in range(blocks):
        pairs_of_refs[number] = (grid_hbm.at[block_at(number)], grid_v.at[block_at(number)])
    pairs_of_refs.update({
        "wkv": (wkv_hbm, wkv_v), "wqd": (wqd_hbm, wqd_v), "dslot": (dslot_hbm, dslot_v), "table": (table_hbm, table_v),
        "wo": (wo_hbm, wo_v), "dgain": (dgain_hbm, dgain_v), "wkvd": (wkvd_hbm, wkvd_v), "wod": (wod_hbm, wod_v),
    })
    loads = {}
    for number, (name, (source, target)) in enumerate(pairs_of_refs.items()):
        loads[name] = pltpu.make_async_copy(source, target, load_sem.at[number])
        loads[name].start()

    def message(kind, source, target, to, leaving, landing):
        return pltpu.make_async_remote_copy(
            src_ref=source,
            dst_ref=target,
            send_sem=send_sem.at[kind, leaving],
            recv_sem=recv_sem.at[kind, landing],
            device_id={"dom": to},
            device_id_type=pl.DeviceIdType.MESH,
        )

    def chip(step):
        return lax.rem(me + 2 * step, peers)

    def need_to(step, slot):
        return message(0, need_v, need_all.at[slot], chip(step), step, slot)

    def edges_to(step, slot):
        return message(1, edges_mine.at[chip(step) // group], edges_all.at[slot], chip(step), step, slot)

    def query_to(step, slot):
        return message(2, query_mine, query_all.at[slot], chip(step), step, slot)

    def mix_to(step, slot):
        return message(3, mix_send.at[step], mix_all.at[slot], chip(step), step, slot)

    def stat_to(step, slot):
        return message(4, stat_send.at[step], stat_all.at[slot], chip(step), step, slot)

    def pairs_to(step, slot):
        return message(5, pairs_all.at[me], pairs_all.at[me], chip(step), step, slot)

    def pairs_on(step, slot):
        owner = chip(step)
        return message(6, pairs_all.at[owner], pairs_all.at[owner], partner, step, slot)

    def push(number):
        return pltpu.make_async_remote_copy(
            src_ref=normed.at[0, block_at(number)],
            dst_ref=normed.at[1, block_at(number)],
            send_sem=push_send.at[number],
            recv_sem=push_recv.at[number],
            device_id={"dom": partner},
            device_id_type=pl.DeviceIdType.MESH,
        )

    others = range(1, chips)

    loads["slot"].wait()
    loads["count"].wait()
    edge_total = slot_v.shape[1]
    own = iota((nodes, nodes), 0) == iota((nodes, nodes), 1)
    counts = jnp.sum(jnp.where(own, count_v[...].astype(F32), 0.0), axis=1, keepdims=True)
    slots = jnp.where(iota(slot_v.shape, 1).astype(F32) < counts, slot_v[...], -1)
    entry = iota((nodes, peers * cap), 1)
    tally = jnp.zeros((nodes, peers * cap), F32)
    for j in range(edge_total):
        tally = tally + jnp.where(slots[:, j : j + 1] == entry, 1.0, 0.0)
    tally = tally.astype(BF16)
    for part in range(peers // group):
        edges_mine[part] = tally[:, part * 128 : (part + 1) * 128]
    edges_all[0] = edges_mine[me // group]
    fan_row = iota((chips * nodes, chips * lanes), 0)
    fan_lane = iota((chips * nodes, chips * lanes), 1)
    fan = fan_row == (fan_lane // lanes) * nodes + lax.rem(fan_lane, nodes)
    fan_of[...] = jnp.where(fan, 1.0, 0.0).astype(BF16)
    loads["need"].wait()
    need_all[0] = need_v[...]
    loads["latent"].wait()
    loads["ngain"].wait()
    loads["wq"].wait()
    queries = jnp.dot(
        norm_into(latent_v[...], ngain_v[...]), wq_v[...], preferred_element_type=F32
    ).astype(BF16)
    query_mine[...] = queries
    query_all[0] = queries

    pl.semaphore_wait(barrier, chips)
    for step in others:
        need_to(step, chips - step).start()
    for step in others:
        edges_to(step, chips - step).start()
        query_to(step, chips - step).start()

    loads["ggain"].wait()
    for number in range(blocks):
        loads[number].wait()

        def norm_block(piece, carry):
            at = pl.ds(pl.multiple_of(number * block + piece * 128, 128), 128)
            normed[0, at, :] = norm_into(grid_v[at, :], ggain_v[...])
            return carry

        lax.fori_loop(0, block // 128, norm_block, 0)
        push(number).start()

    for step in others:
        need_to(step, step).wait_recv()
    base = pl.multiple_of((me // group) * 128, 128)
    lists = need_all[:, :, pl.ds(base, 128)]
    within = lax.rem(me // 2, group // 2) * both
    asked = jnp.broadcast_to(lists, (chips, cap, 128)).astype(F32)
    spot = iota((chips, cap, 128), 1)
    lane = iota((chips, cap, 128), 2)
    wanted = []
    for band in (side, 1 - side):
        picked = jnp.where(lane == within + band * cap + spot, asked, 0.0)
        wanted.append(jnp.sum(picked, axis=2, keepdims=True).astype(jnp.int32).reshape(chips * cap, 1))
    point = iota((chips * cap, points), 1)
    pick = jnp.where(wanted[0] == point, 1.0, 0.0).astype(BF16)
    chosen[: chips * cap] = jnp.dot(pick, normed[0], preferred_element_type=F32).astype(BF16)
    pick = jnp.where(wanted[1] == point, 1.0, 0.0).astype(BF16)
    for number in range(blocks):
        push(number).wait_recv()
    chosen[chips * cap :] = jnp.dot(pick, normed[1], preferred_element_type=F32).astype(BF16)
    loads["wkv"].wait()
    rows[...] = jnp.dot(chosen[...], wkv_v[...], preferred_element_type=F32).astype(BF16)

    for step in others:
        edges_to(step, step).wait_recv()
    spot = iota((both, 128), 0)
    band = jnp.where(spot < cap, side, 1 - side)
    mine = iota((both, 128), 1) == within + band * cap + lax.rem(spot, cap)
    entries = lax.dot_general(
        jnp.where(mine, 1.0, 0.0).astype(BF16), edges_all[...].reshape(chips * nodes, 128), NT,
        preferred_element_type=F32,
    ).astype(BF16)
    entries = jnp.dot(entries, fan_of[...], preferred_element_type=F32)
    for step in others:
        query_to(step, step).wait_recv()

    own_head = iota((lanes, width), 0) // nodes == iota((lanes, width), 1) // head

    def window(w):
        spread_query = jnp.broadcast_to(query_all[w][None], (HEADS, nodes, width)).reshape(lanes, width)
        spread_query = jnp.where(own_head, spread_query, jnp.zeros_like(spread_query))
        near = slice(w * cap, (w + 1) * cap)
        far = slice((chips + w) * cap, (chips + w + 1) * cap)
        keys_here = jnp.concatenate([rows[near, :width], rows[far, :width]], axis=0)
        values_here = jnp.concatenate([rows[near, width:], rows[far, width:]], axis=0)
        scores = lax.dot_general(keys_here, spread_query, NT, preferred_element_type=F32)
        times = entries[:, w * lanes : (w + 1) * lanes]
        scores = jnp.where(times > 0, scores * (1.0 / math.sqrt(head)), -1e30)
        highest = jnp.max(scores, axis=0, keepdims=True)
        raised = jnp.exp(scores - highest) * times
        total = jnp.sum(raised, axis=0, keepdims=True)
        mixed = lax.dot_general(raised.astype(BF16), values_here, TN, preferred_element_type=F32)
        mixed = jnp.where(own_head, mixed, 0.0).reshape(HEADS, nodes, width)
        return jnp.sum(mixed, axis=0).astype(BF16), highest, total

    for step, answer in [(step, window(step)) for step in range(chips)]:
        mixes, stats = (mix_all, stat_all) if step == 0 else (mix_send, stat_send)
        mixes[step] = answer[0]
        stats[step, 0:1, :] = answer[1]
        stats[step, 1:2, :] = answer[2]
    for step in others:
        mix_to(step, chips - step).start()
        stat_to(step, chips - step).start()

    loads["wqd"].wait()
    scale = math.log2(math.e) / math.sqrt(head)
    queries_out[...] = (jnp.dot(normed[0], wqd_v[...], preferred_element_type=F32) * scale).astype(BF16)

    loads["dslot"].wait()
    loads["table"].wait()
    keys = peers * nodes
    dec_cap = table_v.shape[0] * 128 // peers
    slots = dslot_v[...]
    edge_total = slots.shape[0]
    slots = jnp.concatenate([slots] * (8 // edge_total), axis=0)
    columns = []
    for part in range(points // 128):
        piece = slots[:, part * 128 : (part + 1) * 128]
        high = piece // 128
        low = lax.rem(piece, 128)
        need = jnp.zeros_like(piece)
        for line in range(table_v.shape[0]):
            entry = jnp.broadcast_to(table_v[line : line + 1, :], piece.shape)
            need = jnp.where(high == line, jnp.take_along_axis(entry, low, axis=1), need)
        columns.append((piece // dec_cap) * nodes + need)
    node = jnp.concatenate(columns, axis=1)
    times = jnp.ones(node.shape, F32)
    for j in range(1, edge_total):
        times = times + jnp.where(node == jnp.concatenate([node[j:], node[:j]], axis=0), 1.0, 0.0)
    node_of[...] = node.astype(F32).T
    worth_of[...] = jnp.log2(times).T
    name = iota((128, keys), 1).astype(F32)

    def bias_block(piece, carry):
        at = pl.ds(pl.multiple_of(piece * 128, 128), 128)
        nodes_here, worth_here = node_of[at, :], worth_of[at, :]
        bias = jnp.full((128, keys), -1e30, F32)
        for j in range(edge_total):
            bias = jnp.where(nodes_here[:, j : j + 1] == name, worth_here[:, j : j + 1], bias)
        bias_out[at, :] = bias
        return carry

    lax.fori_loop(0, points // 128, bias_block, 0)
    loads["wo"].wait()
    loads["dgain"].wait()
    loads["wkvd"].wait()

    for step in others:
        stat_to(step, step).wait_recv()
    tops = [stat_all[step, 0:1, :] for step in range(chips)]
    sums = [stat_all[step, 1:2, :] for step in range(chips)]
    top = functools.reduce(jnp.maximum, tops)
    shares = [jnp.exp(one - top) for one in tops]
    whole = functools.reduce(jnp.add, [a * b for a, b in zip(shares, sums)])
    own_node = iota((nodes, lanes), 0) == lax.rem(iota((nodes, lanes), 1), nodes)
    stacked = jnp.concatenate([jnp.where(own_node, share / whole, 0.0) for share in shares], axis=0)
    widen = (iota((lanes, width), 0) // nodes == iota((lanes, width), 1) // head).astype(F32)
    factors = jnp.dot(stacked, widen, precision=HIGH, preferred_element_type=F32).reshape(chips, nodes, width)
    for step in others:
        mix_to(step, step).wait_recv()
    enc_mixed = jnp.sum(factors * mix_all[...].astype(F32), axis=0).astype(BF16)
    update = jnp.dot(enc_mixed, wo_v[...], preferred_element_type=F32)
    fresh = (latent_v[...].astype(F32) + update).astype(BF16)
    latent_new[...] = fresh
    pairs = jnp.dot(norm_into(fresh, dgain_v[...]), wkvd_v[...], preferred_element_type=F32).astype(BF16)
    pairs_all[me] = pairs
    for step in others:
        pairs_to(step, chips - step).start()
    pairs_near = message(6, pairs_all.at[me], pairs_all.at[me], partner, 0, 0)
    pairs_near.start()

    for step in others:
        pairs_to(step, step).wait_recv()
        pairs_on(step, step).start()
    pairs_near.wait_recv()
    for step in others:
        pairs_on(step, step).wait_recv()
    pairs_out[...] = pairs_all[...].reshape(pairs_out.shape)

    for step in others:
        for outgoing in (need_to, edges_to, query_to, mix_to, stat_to, pairs_to, pairs_on):
            outgoing(step, step).wait_send()
    pairs_near.wait_send()
    for number in range(blocks):
        push(number).wait_send()
    loads["wod"].wait()


BLOCKS = 4


VMEM_LIMIT = 32 * 1024 * 1024


def encode(grid, latent_in, grid_gain, node_gain, dec_gain, w_q_enc, w_kv_enc, w_o_enc, w_q_dec, w_kv_dec, w_o_dec,
           enc_need, enc_slot, enc_count, dec_slot, dec_need):
    peers = lax.axis_size("dom")
    nodes, model = latent_in.shape
    width = w_q_enc.shape[1]
    entries = enc_need.shape[1]
    cap = entries // peers
    points = grid.shape[0]
    chips = peers // 2
    lanes = HEADS * nodes
    far = pl.BlockSpec(memory_space=pltpu.HBM)
    vmem = pl.BlockSpec(memory_space=pltpu.VMEM)
    operands = (grid, latent_in, grid_gain[None], node_gain[None], dec_gain[None], w_q_enc, w_kv_enc, w_o_enc, w_q_dec,
                w_kv_dec, enc_need, enc_slot.T, enc_count[None], dec_slot, dec_need.reshape(-1, 128), w_o_dec)
    return pl.pallas_call(
        functools.partial(encoder_kernel, peers),
        name="encode",
        out_shape=(
            pltpu.VMEM((nodes, model), BF16),
            pltpu.VMEM((peers * nodes, 2 * width), BF16),
            pltpu.VMEM((points, width), BF16),
            pltpu.VMEM((points, peers * nodes), F32),
            pltpu.VMEM(grid.shape, BF16),
            pltpu.VMEM(w_o_dec.shape, BF16),
        ),
        in_specs=[far] * len(operands),
        out_specs=(vmem,) * 6,
        scratch_shapes=[pltpu.VMEM(one.shape, one.dtype) for one in operands[1:-1]] + [
            pltpu.VMEM((2, points, model), BF16),
            pltpu.VMEM((entries, model), BF16),
            pltpu.VMEM((entries, 2 * width), BF16),
            pltpu.VMEM((chips * nodes, chips * lanes), BF16),
            pltpu.VMEM((nodes, width), BF16),
            pltpu.VMEM((entries // 128, nodes, 128), BF16),
            pltpu.VMEM((chips, 1, entries), jnp.int32),
            pltpu.VMEM((chips, nodes, width), BF16),
            pltpu.VMEM((chips, nodes, 128), BF16),
            pltpu.VMEM((chips, nodes, width), BF16),
            pltpu.VMEM((chips, 2, lanes), F32),
            pltpu.VMEM((chips, nodes, width), BF16),
            pltpu.VMEM((chips, 2, lanes), F32),
            pltpu.VMEM((peers, nodes, 2 * width), BF16),
            pltpu.VMEM((points, 8), F32),
            pltpu.VMEM((points, 8), F32),
            pltpu.SemaphoreType.DMA((len(operands) - 1 + BLOCKS,)),
            pltpu.SemaphoreType.DMA((7, chips)),
            pltpu.SemaphoreType.DMA((7, chips)),
            pltpu.SemaphoreType.DMA((BLOCKS,)),
            pltpu.SemaphoreType.DMA((BLOCKS,)),
        ],
        compiler_params=pltpu.CompilerParams(collective_id=0, has_side_effects=True, vmem_limit_bytes=VMEM_LIMIT),
    )(*[pltpu.with_memory_space_constraint(one, pltpu.HBM) for one in operands])


def decoder_kernel(latent_ref, pairs_v, query_v, bias_v, grid_v, wo_v, latent_hbm, out_hbm,
                   out_v, keys_of, values_of, mixed, store_sem):
    points, width = query_v.shape
    head = width // HEADS
    keys = pairs_v.shape[0]
    quad = 4
    chunks = CHUNKS
    tile = points // chunks

    def rows(part):
        return slice(part * tile, (part + 1) * tile)

    stores = [pltpu.make_async_copy(latent_ref, latent_hbm, store_sem.at[chunks * PIECES])]
    stores[0].start()
    lane_head = iota((keys, quad * head), 1) // head
    for h in range(HEADS):
        some = pairs_v[:, (h // quad) * quad * head : (h // quad + 1) * quad * head]
        keys_of[h] = jnp.where(lane_head == h % quad, some, jnp.zeros_like(some))
    side_of = iota((keys, 2 * head), 1) // head
    for pair in range(HEADS // 2):
        some = pairs_v[:, width + pair * 2 * head : width + (pair + 1) * 2 * head]
        for side in range(2):
            own = side_of == side
            at = slice(side * keys, (side + 1) * keys)
            values_of[pair, at, : 2 * head] = jnp.where(own, some, jnp.zeros_like(some))
            values_of[pair, at, 2 * head :] = jnp.where(own, jnp.ones_like(some), jnp.zeros_like(some))

    for part in range(chunks):
        at = rows(part)
        for pair in range(HEADS // 2):
            four = 2 * pair // quad
            query = query_v[at, four * quad * head : (four + 1) * quad * head]
            raised = []
            for side in range(2):
                scores = lax.dot_general(query, keys_of[2 * pair + side], NT, preferred_element_type=F32)
                scores = scores + bias_v[at, :]
                highest = jnp.max(scores, axis=1, keepdims=True)
                raised.append(jnp.exp2(scores - highest).astype(BF16))
            got = jnp.dot(jnp.concatenate(raised, axis=1), values_of[pair], preferred_element_type=F32)
            mixed[at, pair * 2 * head : (pair + 1) * 2 * head] = (got[:, : 2 * head] / got[:, 2 * head :]).astype(BF16)
        for piece in range(PIECES):
            at = slice(part * tile + piece * (tile // PIECES), part * tile + (piece + 1) * (tile // PIECES))
            update = jnp.dot(mixed[at, :], wo_v[...], preferred_element_type=F32)
            out_v[at, :] = (grid_v[at, :].astype(F32) + update).astype(BF16)
            stores.append(pltpu.make_async_copy(out_v.at[at], out_hbm.at[at], store_sem.at[part * PIECES + piece]))
            stores[-1].start()
    for store in stores:
        store.wait()


CHUNKS = 2
PIECES = 2


def decode(latent_out, pairs, queries, bias, grid, w_o_dec):
    points, model = grid.shape
    width = queries.shape[1]
    keys = pairs.shape[0]
    vmem = pl.BlockSpec(memory_space=pltpu.VMEM)
    far = pl.BlockSpec(memory_space=pltpu.HBM)
    return pl.pallas_call(
        decoder_kernel,
        name="decode",
        out_shape=(
            jax.ShapeDtypeStruct(latent_out.shape, BF16),
            jax.ShapeDtypeStruct(grid.shape, BF16),
        ),
        in_specs=[vmem] * 6,
        out_specs=(far, far),
        scratch_shapes=[
            pltpu.VMEM(grid.shape, BF16),
            pltpu.VMEM((HEADS, keys, width // 2), BF16),
            pltpu.VMEM((HEADS // 2, 2 * keys, 4 * width // HEADS), BF16),
            pltpu.VMEM((points, width), BF16),
            pltpu.SemaphoreType.DMA((CHUNKS * PIECES + 1,)),
        ],
        compiler_params=pltpu.CompilerParams(vmem_limit_bytes=VMEM_LIMIT),
    )(latent_out, pairs, queries, bias, grid, w_o_dec)


def by_kernels(grid, latent_in, grid_gain, node_gain, dec_gain, w_q_enc, w_kv_enc, w_o_enc,
               w_q_dec, w_kv_dec, w_o_dec, enc_need, enc_slot, enc_count, dec_need, dec_slot):
    return decode(*encode(
        grid, latent_in, grid_gain, node_gain, dec_gain, w_q_enc, w_kv_enc, w_o_enc, w_q_dec, w_kv_dec, w_o_dec,
        enc_need, enc_slot, enc_count, dec_slot, dec_need))


def chosen_form(*args):
    grid, latent_in, enc_need, dec_slot = args[0], args[1], args[11], args[15]
    peers = lax.axis_size("dom")
    cap = enc_need.shape[1] // peers
    small = latent_in.shape[0] * peers <= 256
    fits = peers % 2 == 0 and 128 % cap == 0 and cap in (32, 64) and HEADS * latent_in.shape[0] == 128 and grid.shape[0] % 512 == 0
    if small and fits and 8 % dec_slot.shape[0] == 0:
        return by_kernels(*args)
    return on_device(*args)


def solution(mesh):
    both, rep = P(("groups", "dom"), None), P()
    return jax.shard_map(
        chosen_form,
        mesh=mesh,
        in_specs=(both, both, *([rep] * 9), P("dom", None), P(None, "dom"), P("dom"), P("dom", None), P(None, "dom")),
        out_specs=(both, both),
        check_vma=False,
    )
```

```python
import functools
import math

import jax
import jax.numpy as jnp
from jax import lax
from jax.experimental import pallas as pl
from jax.experimental.pallas import tpu as pltpu
from jax.sharding import PartitionSpec as P

HEADS = 8
norm_eps = 1e-06
F32 = jnp.float32
BF16 = jnp.bfloat16


def rms_norm(values, weight_gain):
    widened = values.astype(F32)
    spread = jnp.mean(widened * widened, axis=-1, keepdims=True)
    return (widened * lax.rsqrt(spread + norm_eps) * weight_gain).astype(BF16)


def attend_dense(queries, pairs, edges):
    rows, width = queries.shape
    head = width // HEADS
    q = queries.reshape(rows, HEADS, head)
    k = pairs[:, :width].reshape(-1, HEADS, head)
    v = pairs[:, width:].reshape(-1, HEADS, head)
    scores = jnp.einsum("rhd,khd->hrk", q, k, preferred_element_type=F32)
    scores = jnp.where(edges[None] > 0, scores * (1.0 / math.sqrt(head)), -1e30)
    highest = jnp.max(scores, axis=-1, keepdims=True)
    raised = jnp.exp(scores - highest) * edges[None]
    weights = (raised / jnp.sum(raised, axis=-1, keepdims=True)).astype(BF16)
    mixed = jnp.einsum("hrk,khd->rhd", weights, v, preferred_element_type=F32)
    return mixed.reshape(rows, width).astype(BF16)


def on_device(grid, latent_in, grid_gain, node_gain, dec_gain, w_q_enc, w_kv_enc, w_o_enc,
              w_q_dec, w_kv_dec, w_o_dec, enc_need, enc_slot, enc_count, dec_need, dec_slot):
    peers = lax.axis_size("dom")
    nodes = latent_in.shape[0]
    normed_grid = rms_norm(grid, grid_gain)
    wanted = lax.all_to_all(enc_need.reshape(peers, -1), "dom", split_axis=0, concat_axis=0, tiled=True)
    band = jnp.arange(grid.shape[0], dtype=jnp.int32)
    pick = (wanted.reshape(-1)[:, None] == band[None, :]).astype(BF16)
    chosen = jnp.dot(pick, normed_grid, preferred_element_type=F32).astype(BF16)
    rows = jnp.dot(chosen, w_kv_enc, preferred_element_type=F32).astype(BF16)
    arrived = lax.all_to_all(rows, "dom", split_axis=0, concat_axis=0, tiled=True)
    enc_queries = jnp.dot(rms_norm(latent_in, node_gain), w_q_enc, preferred_element_type=F32).astype(BF16)
    live = jnp.arange(enc_slot.shape[0], dtype=jnp.int32)[:, None] < enc_count[None, :]
    slot_row = jnp.arange(enc_need.shape[1], dtype=jnp.int32)
    enc_edges = jnp.sum((live[:, :, None] & (enc_slot[:, :, None] == slot_row)).astype(F32), axis=0)
    enc_mixed = attend_dense(enc_queries, arrived, enc_edges)
    enc_update = jnp.dot(enc_mixed, w_o_enc, preferred_element_type=F32)
    latent_out = (latent_in.astype(F32) + enc_update).astype(BF16)
    latent_pairs = jnp.dot(rms_norm(latent_out, dec_gain), w_kv_dec, preferred_element_type=F32).astype(BF16)
    dec_queries = jnp.dot(normed_grid, w_q_dec, preferred_element_type=F32).astype(BF16)
    everyone = lax.all_gather(latent_pairs, "dom", axis=0, tiled=True)
    total = dec_need.shape[1]
    cap = total // peers
    lanes = 128
    table = dec_need.reshape(total // lanes, lanes).astype(BF16)
    high = (dec_slot // lanes)[:, :, None] == jnp.arange(total // lanes, dtype=jnp.int32)
    low = (dec_slot % lanes)[:, :, None] == jnp.arange(lanes, dtype=jnp.int32)
    need = jnp.einsum("jgt,tl->jgl", high.astype(BF16), table, preferred_element_type=F32)
    need = jnp.sum(jnp.where(low, need, 0.0), axis=-1).astype(jnp.int32)
    node = (dec_slot // cap) * nodes + need
    dec_edges = jnp.sum((node[:, :, None] == jnp.arange(peers * nodes, dtype=jnp.int32)).astype(F32), axis=0)
    dec_mixed = attend_dense(dec_queries, everyone, dec_edges)
    dec_update = jnp.dot(dec_mixed, w_o_dec, preferred_element_type=F32)
    grid_out = (grid.astype(F32) + dec_update).astype(BF16)
    return (latent_out, grid_out)


NT = (((1,), (1,)), ((), ()))
TN = (((0,), (0,)), ((), ()))
HIGH = lax.Precision.HIGHEST


def iota(shape, dim):
    return lax.broadcasted_iota(jnp.int32, shape, dim)


def norm_into(values, gain):
    widened = values.astype(F32)
    spread = jnp.mean(widened * widened, axis=-1, keepdims=True)
    return (widened * lax.rsqrt(spread + norm_eps) * gain).astype(BF16)


def encoder_kernel(
    peers, grid_hbm, latent_hbm, ggain_hbm, ngain_hbm, dgain_hbm, wq_hbm, wkv_hbm, wo_hbm, wqd_hbm, wkvd_hbm,
    need_hbm, slot_hbm, count_hbm, dslot_hbm, table_hbm, wod_hbm,
    latent_new, pairs_out, queries_out, bias_out, grid_v, wod_v,
    latent_v, ggain_v, ngain_v, dgain_v, wq_v, wkv_v, wo_v, wqd_v, wkvd_v, need_v, slot_v, count_v, dslot_v,
    table_v, normed, band_pairs, rows, query_mine, edges_mine,
    need_all, query_all, edges_all, latents_all, fresh_all, mix_send, stat_send, mix_all, stat_all, mixes_all, pairs_mine, pairs_in,
    node_of, worth_of, load_sem, send_sem, recv_sem, push_send, push_recv, pair_send, pair_recv,
):
    me = lax.axis_index("dom")
    nodes, model = latent_v.shape
    width = wq_v.shape[1]
    head = width // HEADS
    cap = need_v.shape[1] // peers
    group = 128 // cap
    chips = peers // 2
    side = lax.rem(me, 2)
    partner = me + 1 - 2 * side
    points = grid_v.shape[0]
    lanes = HEADS * nodes
    both = 2 * cap
    quad = 4
    here = me // 2
    beside = here + 1 - 2 * lax.rem(here, 2)
    blocks = push_send.shape[0]
    block = points // blocks

    barrier = pltpu.get_barrier_semaphore()
    for to in [lax.rem(me + 2 * step, peers) for step in range(1, chips)] + [partner]:
        pl.semaphore_signal(barrier, inc=1, device_id={"dom": to}, device_id_type=pl.DeviceIdType.MESH)

    def block_at(number):
        return slice(number * block, (number + 1) * block)

    pairs_of_refs = {
        "slot": (slot_hbm, slot_v), "count": (count_hbm, count_v), "need": (need_hbm, need_v),
        "latent": (latent_hbm, latent_v), "ngain": (ngain_hbm, ngain_v), "wq": (wq_hbm, wq_v),
        "ggain": (ggain_hbm, ggain_v),
    }
    for number in range(blocks):
        pairs_of_refs[number] = (grid_hbm.at[block_at(number)], grid_v.at[block_at(number)])
    pairs_of_refs.update({
        "wkv": (wkv_hbm, wkv_v), "wqd": (wqd_hbm, wqd_v), "dslot": (dslot_hbm, dslot_v), "table": (table_hbm, table_v),
        "wo": (wo_hbm, wo_v), "dgain": (dgain_hbm, dgain_v), "wkvd": (wkvd_hbm, wkvd_v), "wod": (wod_hbm, wod_v),
    })
    loads = {}
    for number, (name, (source, target)) in enumerate(pairs_of_refs.items()):
        loads[name] = pltpu.make_async_copy(source, target, load_sem.at[number])
        loads[name].start()

    def message(kind, source, target, to, leaving, landing):
        return pltpu.make_async_remote_copy(
            src_ref=source,
            dst_ref=target,
            send_sem=send_sem.at[kind, leaving],
            recv_sem=recv_sem.at[kind, landing],
            device_id={"dom": to},
            device_id_type=pl.DeviceIdType.MESH,
        )

    def chip(step):
        return lax.rem(me + 2 * step, peers)

    def place(step):
        return lax.rem(here + step, chips)

    def need_to(step, slot):
        return message(0, need_v, need_all.at[slot], chip(step), step, slot)

    def edges_to(step, slot):
        return message(1, edges_mine.at[place(step)], edges_all.at[slot], chip(step), step, slot)

    def query_to(step, slot):
        return message(2, query_mine, query_all.at[slot], chip(step), step, slot)

    def mix_to(step, slot):
        return message(3, mix_send.at[step], mix_all.at[slot], chip(step), step, slot)

    def stat_to(step, slot):
        return message(4, stat_send.at[step], stat_all.at[slot], chip(step), step, slot)

    def mixes_to(step, slot, owner):
        return message(5, mixes_all.at[owner], mixes_all.at[owner], chip(step), step, slot)

    def latent_to(step, slot, owner):
        return message(6, latent_v, latents_all.at[owner], chip(step), step, slot)

    def latent_beside(owner):
        return message(6, latent_v, latents_all.at[owner], 2 * beside + side, 1, 1)

    def latent_on(step, owner):
        return message(7, latents_all.at[owner], latents_all.at[owner], 2 * beside + side, step, step)

    def pair_over(number):
        return pltpu.make_async_remote_copy(
            src_ref=pairs_mine.at[number],
            dst_ref=pairs_in.at[number],
            send_sem=pair_send.at[number],
            recv_sem=pair_recv.at[number],
            device_id={"dom": partner},
            device_id_type=pl.DeviceIdType.MESH,
        )

    def push(number):
        return pltpu.make_async_remote_copy(
            src_ref=band_pairs.at[0, block_at(number)],
            dst_ref=band_pairs.at[1, block_at(number)],
            send_sem=push_send.at[number],
            recv_sem=push_recv.at[number],
            device_id={"dom": partner},
            device_id_type=pl.DeviceIdType.MESH,
        )

    others = [step for low in range(1, chips // 2) for step in (low, chips - low)] + [chips // 2]
    alike = range(2, chips, 2)

    loads["slot"].wait()
    loads["count"].wait()
    edge_total = slot_v.shape[1]
    own = iota((nodes, nodes), 0) == iota((nodes, nodes), 1)
    counts = jnp.sum(jnp.where(own, count_v[...].astype(F32), 0.0), axis=1, keepdims=True)
    slots = jnp.where(iota(slot_v.shape, 1).astype(F32) < counts, slot_v[...], -1)
    entry = iota((nodes, peers * cap), 1)
    tally = jnp.zeros((nodes, peers * cap), F32)
    for j in range(edge_total):
        tally = tally + jnp.where(slots[:, j : j + 1] == entry, 1.0, 0.0)
    tally = tally.astype(BF16)
    for number in range(chips):
        own_part = tally[:, number * both : (number + 1) * both]
        edges_mine[number] = jnp.concatenate([own_part] * (128 // both), axis=1)
    edges_all[0] = edges_mine[here]
    loads["need"].wait()
    need_all[0] = need_v[...]
    loads["latent"].wait()
    loads["ngain"].wait()
    loads["wq"].wait()
    queries = jnp.dot(
        norm_into(latent_v[...], ngain_v[...]), wq_v[...], preferred_element_type=F32
    ).astype(BF16)
    query_mine[...] = queries
    query_all[0] = queries
    latents_all[here] = latent_v[...]

    pl.semaphore_wait(barrier, chips)
    for step in others:
        need_to(step, chips - step).start()
    for step in others:
        edges_to(step, chips - step).start()
        query_to(step, chips - step).start()

    loads["ggain"].wait()
    for number in range(blocks):
        loads[number].wait()
    loads["wkv"].wait()
    settled = norm_into(grid_v[block_at(0), :], ggain_v[...])
    for number in range(blocks):
        at = block_at(number)
        normed[at, :] = settled
        band_pairs[0, at, :] = jnp.dot(settled, wkv_v[...], preferred_element_type=F32).astype(BF16)
        if number + 1 < blocks:
            settled = norm_into(grid_v[block_at(number + 1), :], ggain_v[...])
        push(number).start()
    for step in alike:
        latent_to(step, chips - step, here).start()
    latent_beside(here).start()

    for step in others:
        need_to(step, step).wait_recv()
    base = pl.multiple_of((me // group) * 128, 128)
    lists = need_all[:, :, pl.ds(base, 128)]
    within = lax.rem(me // 2, group // 2) * both
    asked = jnp.broadcast_to(lists, (chips, cap, 128)).astype(F32)
    spot = iota((chips, cap, 128), 1)
    lane = iota((chips, cap, 128), 2)
    wanted = []
    for band in (side, 1 - side):
        picked = jnp.where(lane == within + band * cap + spot, asked, 0.0)
        wanted.append(jnp.sum(picked, axis=2, keepdims=True).astype(jnp.int32).reshape(chips * cap, 1))
    point = iota((chips * cap, points), 1)
    def rows_of(band):
        pick = jnp.where(wanted[band] == point, 1.0, 0.0).astype(BF16)
        return jnp.dot(pick, band_pairs[band], preferred_element_type=F32).astype(BF16)

    rows[side] = rows_of(0)
    for number in range(blocks):
        push(number).wait_recv()
    rows[1 - side] = rows_of(1)

    for step in others:
        edges_to(step, step).wait_recv()
        query_to(step, step).wait_recv()

    scale = math.log2(math.e) / math.sqrt(head)
    span = quad * head
    own_head = iota((quad * nodes, span), 0) // nodes == iota((quad * nodes, span), 1) // head
    tasks = [(step, four) for step in range(chips) for four in range(HEADS // quad)]

    def score(step, four):
        lane = slice(four * span, (four + 1) * span)
        at = slice(step * cap, (step + 1) * cap)
        query = jnp.concatenate([query_all[step][:, lane]] * quad, axis=0)
        query = jnp.where(own_head, query, jnp.zeros_like(query))
        keys_here = jnp.concatenate([rows[0, at, lane], rows[1, at, lane]], axis=0)
        return lax.dot_general(query, keys_here, NT, preferred_element_type=F32)

    def soften(step, scores):
        times = jnp.concatenate([edges_all[step][:, :both].astype(F32)] * quad, axis=0)
        scores = jnp.where(times > 0, scores * scale, -1e30)
        highest = jnp.max(scores, axis=1, keepdims=True)
        raised = jnp.exp2(scores - highest) * times
        return raised.astype(BF16), jnp.broadcast_to(highest, (quad * nodes, 128))

    def blend(step, four, raised):
        lane = slice(width + four * span, width + (four + 1) * span)
        at = slice(step * cap, (step + 1) * cap)
        values_here = jnp.concatenate([rows[0, at, lane], rows[1, at, lane]], axis=0)
        mixed = jnp.dot(raised, values_here, preferred_element_type=F32)
        mixed = jnp.where(own_head, mixed, 0.0)
        return functools.reduce(jnp.add, [mixed[j * nodes : (j + 1) * nodes] for j in range(quad)]).astype(BF16)

    stat_lane = iota((lanes, 128), 1)
    board = jnp.zeros((lanes, 128), F32)
    every = jnp.ones((both, 128), BF16)
    for first in range(0, len(tasks), WAVE):
        wave = tasks[first : first + WAVE]
        scored = [score(step, four) for step, four in wave]
        softened = [soften(step, one) for (step, four), one in zip(wave, scored)]
        for (step, four), one in zip(wave, softened):
            mixes = mix_all if step == 0 else mix_send
            mixes[step, :, four * span : (four + 1) * span] = blend(step, four, one[0])
        for number in range(0, len(wave), HEADS // quad):
            step = wave[number][0]
            group_of = softened[number : number + HEADS // quad]
            totals = [jnp.dot(one[0], every, preferred_element_type=F32) for one in group_of]
            board = jnp.where(stat_lane == step, jnp.concatenate([one[1] for one in group_of], axis=0), board)
            board = jnp.where(stat_lane == chips + step, jnp.concatenate(totals, axis=0), board)
    board = board.T
    for step in range(chips):
        stats = stat_all if step == 0 else stat_send
        stats[step, 0:1, :] = board[step : step + 1]
        stats[step, 1:2, :] = board[chips + step : chips + step + 1]
    for step in others:
        mix_to(step, chips - step).start()
        stat_to(step, chips - step).start()

    for step in alike:
        latent_to(step, step, place(step)).wait_recv()
        latent_on(step, place(step)).start()

    loads["wqd"].wait()
    queries_out[...] = (jnp.dot(normed[...], wqd_v[...], preferred_element_type=F32) * scale).astype(BF16)

    loads["wo"].wait()
    loads["dgain"].wait()
    loads["wkvd"].wait()

    for step in others:
        stat_to(step, step).wait_recv()
    tops = [stat_all[step, 0:1, :] for step in range(chips)]
    sums = [stat_all[step, 1:2, :] for step in range(chips)]
    top = functools.reduce(jnp.maximum, tops)
    shares = [jnp.exp2(one - top) for one in tops]
    whole = functools.reduce(jnp.add, [a * b for a, b in zip(shares, sums)])
    own_node = iota((nodes, lanes), 0) == lax.rem(iota((nodes, lanes), 1), nodes)
    stacked = jnp.concatenate([jnp.where(own_node, share / whole, 0.0) for share in shares], axis=0)
    widen = (iota((lanes, width), 0) // nodes == iota((lanes, width), 1) // head).astype(F32)
    factors = jnp.dot(stacked, widen, precision=HIGH, preferred_element_type=F32).reshape(chips, nodes, width)
    for step in others:
        mix_to(step, step).wait_recv()
    enc_mixed = jnp.sum(factors * mix_all[...].astype(F32), axis=0).astype(BF16)
    mixes_all[here] = enc_mixed
    for step in others:
        mixes_to(step, chips - step, here).start()

    loads["dslot"].wait()
    loads["table"].wait()
    keys = peers * nodes
    dec_cap = table_v.shape[0] * 128 // peers
    slots = dslot_v[...]
    edge_total = slots.shape[0]
    slots = jnp.concatenate([slots] * (8 // edge_total), axis=0)
    columns = []
    for part in range(points // 128):
        piece = slots[:, part * 128 : (part + 1) * 128]
        high = piece // 128
        low = lax.rem(piece, 128)
        need = jnp.zeros_like(piece)
        for line in range(table_v.shape[0]):
            entry = jnp.broadcast_to(table_v[line : line + 1, :], piece.shape)
            need = jnp.where(high == line, jnp.take_along_axis(entry, low, axis=1), need)
        owner = piece // dec_cap
        columns.append(lax.rem(owner, 2) * (chips * nodes) + (owner // 2) * nodes + need)
    node = jnp.concatenate(columns, axis=1)
    times = jnp.ones(node.shape, F32)
    for j in range(1, edge_total):
        times = times + jnp.where(node == jnp.concatenate([node[j:], node[:j]], axis=0), 1.0, 0.0)
    node_of[...] = node.astype(F32).T
    worth_of[...] = jnp.log2(times).T
    name = iota((128, keys), 1).astype(F32)

    def bias_block(piece, carry):
        at = pl.ds(pl.multiple_of(piece * 128, 128), 128)
        nodes_here, worth_here = node_of[at, :], worth_of[at, :]
        bias = jnp.full((128, keys), -1e30, F32)
        for j in range(edge_total):
            bias = jnp.where(nodes_here[:, j : j + 1] == name, worth_here[:, j : j + 1], bias)
        bias_out[at, :] = bias
        return carry

    lax.fori_loop(0, points // 128, bias_block, 0)

    latent_beside(beside).wait_recv()
    for step in alike:
        latent_on(step, lax.rem(beside + step, chips)).wait_recv()
    for step in others:
        mixes_to(step, step, place(step)).wait_recv()
    side_nodes = chips * nodes
    update = jnp.dot(mixes_all[...].reshape(side_nodes, width), wo_v[...], preferred_element_type=F32)
    fresh = (latents_all[...].reshape(side_nodes, model).astype(F32) + update).astype(BF16)
    fresh_all[...] = fresh.reshape(chips, nodes, model)
    settled = norm_into(fresh, dgain_v[...])
    for number in range(2):
        half = jnp.dot(settled, wkvd_v[:, number * width : (number + 1) * width], preferred_element_type=F32).astype(BF16)
        pairs_mine[number] = half
        pair_over(number).start()
    latent_new[...] = fresh_all[here]
    near = pl.ds(pl.multiple_of(side * side_nodes, side_nodes), side_nodes)
    over = pl.ds(pl.multiple_of((1 - side) * side_nodes, side_nodes), side_nodes)
    for number in range(2):
        pairs_out[number, near, :] = pairs_mine[number]
    for number in range(2):
        pair_over(number).wait_recv()
        pairs_out[number, over, :] = pairs_in[number]

    for step in others:
        for outgoing in (need_to, edges_to, query_to, mix_to, stat_to):
            outgoing(step, step).wait_send()
        mixes_to(step, step, here).wait_send()
    for step in alike:
        latent_to(step, step, here).wait_send()
        latent_on(step, place(step)).wait_send()
    latent_beside(here).wait_send()
    for number in range(blocks):
        push(number).wait_send()
    for number in range(2):
        pair_over(number).wait_send()
    loads["wod"].wait()


WAVE = 16
BLOCKS = 4


VMEM_LIMIT = 32 * 1024 * 1024


def encode(grid, latent_in, grid_gain, node_gain, dec_gain, w_q_enc, w_kv_enc, w_o_enc, w_q_dec, w_kv_dec, w_o_dec,
           enc_need, enc_slot, enc_count, dec_slot, dec_need):
    peers = lax.axis_size("dom")
    nodes, model = latent_in.shape
    width = w_q_enc.shape[1]
    entries = enc_need.shape[1]
    cap = entries // peers
    points = grid.shape[0]
    chips = peers // 2
    lanes = HEADS * nodes
    far = pl.BlockSpec(memory_space=pltpu.HBM)
    vmem = pl.BlockSpec(memory_space=pltpu.VMEM)
    operands = (grid, latent_in, grid_gain[None], node_gain[None], dec_gain[None], w_q_enc, w_kv_enc, w_o_enc, w_q_dec,
                w_kv_dec, enc_need, enc_slot.T, enc_count[None], dec_slot, dec_need.reshape(-1, 128), w_o_dec)
    return pl.pallas_call(
        functools.partial(encoder_kernel, peers),
        name="encode",
        out_shape=(
            pltpu.VMEM((nodes, model), BF16),
            pltpu.VMEM((2, peers * nodes, width), BF16),
            pltpu.VMEM((points, width), BF16),
            pltpu.VMEM((points, peers * nodes), F32),
            pltpu.VMEM(grid.shape, BF16),
            pltpu.VMEM(w_o_dec.shape, BF16),
        ),
        in_specs=[far] * len(operands),
        out_specs=(vmem,) * 6,
        scratch_shapes=[pltpu.VMEM(one.shape, one.dtype) for one in operands[1:-1]] + [
            pltpu.VMEM((points, model), BF16),
            pltpu.VMEM((2, points, 2 * width), BF16),
            pltpu.VMEM((2, chips * cap, 2 * width), BF16),
            pltpu.VMEM((nodes, width), BF16),
            pltpu.VMEM((chips, nodes, 128), BF16),
            pltpu.VMEM((chips, 1, entries), jnp.int32),
            pltpu.VMEM((chips, nodes, width), BF16),
            pltpu.VMEM((chips, nodes, 128), BF16),
            pltpu.VMEM((chips, nodes, model), BF16),
            pltpu.VMEM((chips, nodes, model), BF16),
            pltpu.VMEM((chips, nodes, width), BF16),
            pltpu.VMEM((chips, 2, lanes), F32),
            pltpu.VMEM((chips, nodes, width), BF16),
            pltpu.VMEM((chips, 2, lanes), F32),
            pltpu.VMEM((chips, nodes, width), BF16),
            pltpu.VMEM((2, chips * nodes, width), BF16),
            pltpu.VMEM((2, chips * nodes, width), BF16),
            pltpu.VMEM((points, 8), F32),
            pltpu.VMEM((points, 8), F32),
            pltpu.SemaphoreType.DMA((len(operands) - 1 + BLOCKS,)),
            pltpu.SemaphoreType.DMA((8, chips)),
            pltpu.SemaphoreType.DMA((8, chips)),
            pltpu.SemaphoreType.DMA((BLOCKS,)),
            pltpu.SemaphoreType.DMA((BLOCKS,)),
            pltpu.SemaphoreType.DMA((2,)),
            pltpu.SemaphoreType.DMA((2,)),
        ],
        compiler_params=pltpu.CompilerParams(collective_id=0, has_side_effects=True, vmem_limit_bytes=VMEM_LIMIT),
    )(*[pltpu.with_memory_space_constraint(one, pltpu.HBM) for one in operands])


def decoder_kernel(latent_ref, pairs_v, query_v, bias_v, grid_v, wo_v, latent_hbm, out_hbm,
                   out_v, keys_of, values_of, mixed, store_sem):
    points, width = query_v.shape
    head = width // HEADS
    keys = pairs_v.shape[1]
    quad = 4
    chunks = CHUNKS
    tile = points // chunks

    def rows(part):
        return slice(part * tile, (part + 1) * tile)

    stores = [pltpu.make_async_copy(latent_ref, latent_hbm, store_sem.at[chunks * PIECES])]
    stores[0].start()
    lane_head = iota((keys, quad * head), 1) // head
    for h in range(HEADS):
        some = pairs_v[0, :, (h // quad) * quad * head : (h // quad + 1) * quad * head]
        keys_of[h] = jnp.where(lane_head == h % quad, some, jnp.zeros_like(some))
    side_of = iota((keys, 2 * head), 1) // head
    for pair in range(HEADS // 2):
        some = pairs_v[1, :, pair * 2 * head : (pair + 1) * 2 * head]
        for side in range(2):
            own = side_of == side
            at = slice(side * keys, (side + 1) * keys)
            values_of[pair, at, : 2 * head] = jnp.where(own, some, jnp.zeros_like(some))
            values_of[pair, at, 2 * head :] = jnp.where(own, jnp.ones_like(some), jnp.zeros_like(some))

    for part in range(chunks):
        at = rows(part)
        for pair in range(HEADS // 2):
            four = 2 * pair // quad
            query = query_v[at, four * quad * head : (four + 1) * quad * head]
            raised = []
            for side in range(2):
                scores = lax.dot_general(query, keys_of[2 * pair + side], NT, preferred_element_type=F32)
                scores = scores + bias_v[at, :]
                highest = jnp.max(scores, axis=1, keepdims=True)
                raised.append(jnp.exp2(scores - highest).astype(BF16))
            got = jnp.dot(jnp.concatenate(raised, axis=1), values_of[pair], preferred_element_type=F32)
            mixed[at, pair * 2 * head : (pair + 1) * 2 * head] = (got[:, : 2 * head] / got[:, 2 * head :]).astype(BF16)
        for piece in range(PIECES):
            at = slice(part * tile + piece * (tile // PIECES), part * tile + (piece + 1) * (tile // PIECES))
            update = jnp.dot(mixed[at, :], wo_v[...], preferred_element_type=F32)
            out_v[at, :] = (grid_v[at, :].astype(F32) + update).astype(BF16)
            stores.append(pltpu.make_async_copy(out_v.at[at], out_hbm.at[at], store_sem.at[part * PIECES + piece]))
            stores[-1].start()
    for store in stores:
        store.wait()


CHUNKS = 2
PIECES = 2


def decode(latent_out, pairs, queries, bias, grid, w_o_dec):
    points, model = grid.shape
    width = queries.shape[1]
    keys = pairs.shape[1]
    vmem = pl.BlockSpec(memory_space=pltpu.VMEM)
    far = pl.BlockSpec(memory_space=pltpu.HBM)
    return pl.pallas_call(
        decoder_kernel,
        name="decode",
        out_shape=(
            jax.ShapeDtypeStruct(latent_out.shape, BF16),
            jax.ShapeDtypeStruct(grid.shape, BF16),
        ),
        in_specs=[vmem] * 6,
        out_specs=(far, far),
        scratch_shapes=[
            pltpu.VMEM(grid.shape, BF16),
            pltpu.VMEM((HEADS, keys, width // 2), BF16),
            pltpu.VMEM((HEADS // 2, 2 * keys, 4 * width // HEADS), BF16),
            pltpu.VMEM((points, width), BF16),
            pltpu.SemaphoreType.DMA((CHUNKS * PIECES + 1,)),
        ],
        compiler_params=pltpu.CompilerParams(vmem_limit_bytes=VMEM_LIMIT),
    )(latent_out, pairs, queries, bias, grid, w_o_dec)


def by_kernels(grid, latent_in, grid_gain, node_gain, dec_gain, w_q_enc, w_kv_enc, w_o_enc,
               w_q_dec, w_kv_dec, w_o_dec, enc_need, enc_slot, enc_count, dec_need, dec_slot):
    return decode(*encode(
        grid, latent_in, grid_gain, node_gain, dec_gain, w_q_enc, w_kv_enc, w_o_enc, w_q_dec, w_kv_dec, w_o_dec,
        enc_need, enc_slot, enc_count, dec_slot, dec_need))


def chosen_form(*args):
    grid, latent_in, enc_need, dec_slot = args[0], args[1], args[11], args[15]
    peers = lax.axis_size("dom")
    cap = enc_need.shape[1] // peers
    small = latent_in.shape[0] * peers <= 256
    fits = peers % 4 == 0 and 128 % cap == 0 and cap in (32, 64) and peers <= 128 and HEADS * latent_in.shape[0] == 128 and grid.shape[0] % 512 == 0
    if small and fits and 8 % dec_slot.shape[0] == 0:
        return by_kernels(*args)
    return on_device(*args)


def solution(mesh):
    both, rep = P(("groups", "dom"), None), P()
    return jax.shard_map(
        chosen_form,
        mesh=mesh,
        in_specs=(both, both, *([rep] * 9), P("dom", None), P(None, "dom"), P("dom"), P("dom", None), P(None, "dom")),
        out_specs=(both, both),
        check_vma=False,
    )
```

```python
import functools
import math

import jax
import jax.numpy as jnp
from jax import lax
from jax.experimental import pallas as pl
from jax.experimental.pallas import tpu as pltpu
from jax.sharding import PartitionSpec as P

HEADS = 8
norm_eps = 1e-06
F32 = jnp.float32
BF16 = jnp.bfloat16


def rms_norm(values, weight_gain):
    widened = values.astype(F32)
    spread = jnp.mean(widened * widened, axis=-1, keepdims=True)
    return (widened * lax.rsqrt(spread + norm_eps) * weight_gain).astype(BF16)


def attend_dense(queries, pairs, edges):
    rows, width = queries.shape
    head = width // HEADS
    q = queries.reshape(rows, HEADS, head)
    k = pairs[:, :width].reshape(-1, HEADS, head)
    v = pairs[:, width:].reshape(-1, HEADS, head)
    scores = jnp.einsum("rhd,khd->hrk", q, k, preferred_element_type=F32)
    scores = jnp.where(edges[None] > 0, scores * (1.0 / math.sqrt(head)), -1e30)
    highest = jnp.max(scores, axis=-1, keepdims=True)
    raised = jnp.exp(scores - highest) * edges[None]
    weights = (raised / jnp.sum(raised, axis=-1, keepdims=True)).astype(BF16)
    mixed = jnp.einsum("hrk,khd->rhd", weights, v, preferred_element_type=F32)
    return mixed.reshape(rows, width).astype(BF16)


def on_device(grid, latent_in, grid_gain, node_gain, dec_gain, w_q_enc, w_kv_enc, w_o_enc,
              w_q_dec, w_kv_dec, w_o_dec, enc_need, enc_slot, enc_count, dec_need, dec_slot):
    peers = lax.axis_size("dom")
    nodes = latent_in.shape[0]
    normed_grid = rms_norm(grid, grid_gain)
    wanted = lax.all_to_all(enc_need.reshape(peers, -1), "dom", split_axis=0, concat_axis=0, tiled=True)
    band = jnp.arange(grid.shape[0], dtype=jnp.int32)
    pick = (wanted.reshape(-1)[:, None] == band[None, :]).astype(BF16)
    chosen = jnp.dot(pick, normed_grid, preferred_element_type=F32).astype(BF16)
    rows = jnp.dot(chosen, w_kv_enc, preferred_element_type=F32).astype(BF16)
    arrived = lax.all_to_all(rows, "dom", split_axis=0, concat_axis=0, tiled=True)
    enc_queries = jnp.dot(rms_norm(latent_in, node_gain), w_q_enc, preferred_element_type=F32).astype(BF16)
    live = jnp.arange(enc_slot.shape[0], dtype=jnp.int32)[:, None] < enc_count[None, :]
    slot_row = jnp.arange(enc_need.shape[1], dtype=jnp.int32)
    enc_edges = jnp.sum((live[:, :, None] & (enc_slot[:, :, None] == slot_row)).astype(F32), axis=0)
    enc_mixed = attend_dense(enc_queries, arrived, enc_edges)
    enc_update = jnp.dot(enc_mixed, w_o_enc, preferred_element_type=F32)
    latent_out = (latent_in.astype(F32) + enc_update).astype(BF16)
    latent_pairs = jnp.dot(rms_norm(latent_out, dec_gain), w_kv_dec, preferred_element_type=F32).astype(BF16)
    dec_queries = jnp.dot(normed_grid, w_q_dec, preferred_element_type=F32).astype(BF16)
    everyone = lax.all_gather(latent_pairs, "dom", axis=0, tiled=True)
    total = dec_need.shape[1]
    cap = total // peers
    lanes = 128
    table = dec_need.reshape(total // lanes, lanes).astype(BF16)
    high = (dec_slot // lanes)[:, :, None] == jnp.arange(total // lanes, dtype=jnp.int32)
    low = (dec_slot % lanes)[:, :, None] == jnp.arange(lanes, dtype=jnp.int32)
    need = jnp.einsum("jgt,tl->jgl", high.astype(BF16), table, preferred_element_type=F32)
    need = jnp.sum(jnp.where(low, need, 0.0), axis=-1).astype(jnp.int32)
    node = (dec_slot // cap) * nodes + need
    dec_edges = jnp.sum((node[:, :, None] == jnp.arange(peers * nodes, dtype=jnp.int32)).astype(F32), axis=0)
    dec_mixed = attend_dense(dec_queries, everyone, dec_edges)
    dec_update = jnp.dot(dec_mixed, w_o_dec, preferred_element_type=F32)
    grid_out = (grid.astype(F32) + dec_update).astype(BF16)
    return (latent_out, grid_out)


NT = (((1,), (1,)), ((), ()))
TN = (((0,), (0,)), ((), ()))
HIGH = lax.Precision.HIGHEST


def iota(shape, dim):
    return lax.broadcasted_iota(jnp.int32, shape, dim)


def norm_into(values, gain):
    widened = values.astype(F32)
    spread = jnp.mean(widened * widened, axis=-1, keepdims=True)
    return (widened * lax.rsqrt(spread + norm_eps) * gain).astype(BF16)


def encoder_kernel(
    peers, grid_hbm, latent_hbm, ggain_hbm, ngain_hbm, dgain_hbm, wq_hbm, wkv_hbm, wo_hbm, wqd_hbm, wkvd_hbm,
    need_hbm, slot_hbm, count_hbm, dslot_hbm, table_hbm, wod_hbm,
    latent_new, pairs_out, queries_out, bias_out, grid_v, wod_v,
    latent_v, ggain_v, ngain_v, dgain_v, wq_v, wkv_v, wo_v, wqd_v, wkvd_v, need_v, slot_v, count_v, dslot_v,
    table_v, normed, band_pairs, rows, query_mine, edges_mine,
    need_all, query_all, edges_all, latents_all, mix_send, stat_send, mix_all, stat_all, mixes_all, pairs_mine, pairs_in,
    node_of, worth_of, load_sem, send_sem, recv_sem, push_sem, pair_send, pair_recv,
):
    me = lax.axis_index("dom")
    nodes, model = latent_v.shape
    width = wq_v.shape[1]
    head = width // HEADS
    cap = need_v.shape[1] // peers
    group = 128 // cap
    chips = peers // 2
    side = lax.rem(me, 2)
    partner = me + 1 - 2 * side
    points = grid_v.shape[0]
    lanes = HEADS * nodes
    both = 2 * cap
    quad = 4
    here = me // 2
    beside = here + 1 - 2 * lax.rem(here, 2)
    blocks = BLOCKS
    block = points // blocks

    barrier = pltpu.get_barrier_semaphore()
    for to in [lax.rem(me + 2 * step, peers) for step in range(1, chips)] + [partner]:
        pl.semaphore_signal(barrier, inc=1, device_id={"dom": to}, device_id_type=pl.DeviceIdType.MESH)

    def block_at(number):
        return slice(number * block, (number + 1) * block)

    pairs_of_refs = {
        "slot": (slot_hbm, slot_v), "count": (count_hbm, count_v), "need": (need_hbm, need_v),
        "latent": (latent_hbm, latent_v), "ngain": (ngain_hbm, ngain_v), "wq": (wq_hbm, wq_v),
        "ggain": (ggain_hbm, ggain_v),
    }
    for number in range(blocks):
        pairs_of_refs[number] = (grid_hbm.at[block_at(number)], grid_v.at[block_at(number)])
    pairs_of_refs.update({
        "wkv": (wkv_hbm, wkv_v), "wqd": (wqd_hbm, wqd_v), "dslot": (dslot_hbm, dslot_v), "table": (table_hbm, table_v),
        "wo": (wo_hbm, wo_v), "dgain": (dgain_hbm, dgain_v), "wkvd": (wkvd_hbm, wkvd_v), "wod": (wod_hbm, wod_v),
    })
    loads = {}
    for number, (name, (source, target)) in enumerate(pairs_of_refs.items()):
        loads[name] = pltpu.make_async_copy(source, target, load_sem.at[number])
        loads[name].start()

    def message(kind, source, target, to, landing=None):
        return pltpu.make_async_remote_copy(
            src_ref=source,
            dst_ref=target,
            send_sem=send_sem.at[kind],
            recv_sem=recv_sem.at[kind if landing is None else landing],
            device_id={"dom": to},
            device_id_type=pl.DeviceIdType.MESH,
        )

    def chip(step):
        return lax.rem(me + 2 * step, peers)

    def place(step):
        return lax.rem(here + step, chips)

    def exchange(kind, buffer):
        rest = buffer.at[pl.ds(1, chips - 1)]
        return message(kind, rest, rest, partner)

    def need_to(step):
        return message(0, need_v, need_all.at[chips - step], chip(step))

    def edges_to(step):
        return message(1, edges_mine.at[place(step)], edges_all.at[chips - step], chip(step))

    def query_to(step):
        return message(2, query_mine, query_all.at[chips - step], chip(step))

    def mix_to(step):
        return message(3, mix_send.at[step], mix_all.at[chips - step], chip(step))

    def stat_to(step):
        return message(4, stat_send.at[step], stat_all.at[chips - step], chip(step))

    def mixes_to(step):
        return message(5, mixes_all.at[0], mixes_all.at[chips - step], chip(step))

    apart = chips + here - beside

    def latent_to(step, slot):
        return message(6, latents_all.at[0], latents_all.at[slot], chip(step), 6 + slot // 2)

    def latent_from(slot):
        return message(6, latents_all.at[slot], latents_all.at[slot], partner, 6 + slot // 2)

    def latent_on(slot):
        return message(
            6, latents_all.at[slot], latents_all.at[lax.rem(slot + apart, chips)], 2 * beside + side, 6
        )

    def latents_beside():
        some = latents_all.at[pl.ds(0, chips // 2)]
        return message(6, some, some, partner, 6)

    push_whole = pltpu.make_async_remote_copy(
        src_ref=band_pairs.at[0],
        dst_ref=band_pairs.at[1],
        send_sem=push_sem.at[0],
        recv_sem=push_sem.at[1],
        device_id={"dom": partner},
        device_id_type=pl.DeviceIdType.MESH,
    )

    def pair_over(number):
        return pltpu.make_async_remote_copy(
            src_ref=pairs_mine.at[number],
            dst_ref=pairs_in.at[number],
            send_sem=pair_send.at[number],
            recv_sem=pair_recv.at[number],
            device_id={"dom": partner},
            device_id_type=pl.DeviceIdType.MESH,
        )

    def push(number):
        return pltpu.make_async_remote_copy(
            src_ref=band_pairs.at[0, block_at(number)],
            dst_ref=band_pairs.at[1, block_at(number)],
            send_sem=push_sem.at[0],
            recv_sem=push_sem.at[1],
            device_id={"dom": partner},
            device_id_type=pl.DeviceIdType.MESH,
        )

    others = [step for low in range(1, chips // 2) for step in (low, chips - low)] + [chips // 2]
    alike = range(2, chips, 2)

    loads["slot"].wait()
    loads["count"].wait()
    edge_total = slot_v.shape[1]
    own = iota((nodes, nodes), 0) == iota((nodes, nodes), 1)
    counts = jnp.sum(jnp.where(own, count_v[...].astype(F32), 0.0), axis=1, keepdims=True)
    slots = jnp.where(iota(slot_v.shape, 1).astype(F32) < counts, slot_v[...], -1)
    entry = iota((nodes, peers * cap), 1)
    tally = jnp.zeros((nodes, peers * cap), F32)
    for j in range(edge_total):
        tally = tally + jnp.where(slots[:, j : j + 1] == entry, 1.0, 0.0)
    tally = tally.astype(BF16)
    for number in range(chips):
        own_part = tally[:, number * both : (number + 1) * both]
        edges_mine[number] = jnp.concatenate([own_part] * (128 // both), axis=1)
    edges_all[0] = edges_mine[here]
    loads["need"].wait()
    need_all[0] = need_v[...]
    loads["latent"].wait()
    loads["ngain"].wait()
    loads["wq"].wait()
    queries = jnp.dot(
        norm_into(latent_v[...], ngain_v[...]), wq_v[...], preferred_element_type=F32
    ).astype(BF16)
    query_mine[...] = queries
    query_all[0] = queries
    latents_all[0] = latent_v[...]

    pl.semaphore_wait(barrier, chips)
    for step in others:
        need_to(step).start()
    for step in others:
        edges_to(step).start()
        query_to(step).start()

    loads["ggain"].wait()
    for number in range(blocks):
        loads[number].wait()
    loads["wkv"].wait()
    settled = norm_into(grid_v[block_at(0), :], ggain_v[...])
    for number in range(blocks):
        at = block_at(number)
        normed[at, :] = settled
        band_pairs[0, at, :] = jnp.dot(settled, wkv_v[...], preferred_element_type=F32).astype(BF16)
        if number + 1 < blocks:
            settled = norm_into(grid_v[block_at(number + 1), :], ggain_v[...])
        push(number).start()
    for step in alike:
        latent_to(step, chips - step).start()
    latent_on(0).start()

    exchange(0, need_all).wait_recv()
    base = pl.multiple_of((me // group) * 128, 128)
    lists = need_all[:, :, pl.ds(base, 128)]
    within = lax.rem(me // 2, group // 2) * both
    asked = jnp.broadcast_to(lists, (chips, cap, 128)).astype(F32)
    spot = iota((chips, cap, 128), 1)
    lane = iota((chips, cap, 128), 2)
    wanted = []
    for band in (side, 1 - side):
        picked = jnp.where(lane == within + band * cap + spot, asked, 0.0)
        wanted.append(jnp.sum(picked, axis=2, keepdims=True).astype(jnp.int32).reshape(chips * cap, 1))
    point = iota((chips * cap, points), 1)
    def pick_of(band):
        return jnp.where(wanted[band] == point, 1.0, 0.0).astype(BF16)

    def rows_of(band, part):
        lane = slice(part * width, (part + 1) * width)
        return jnp.dot(pick_of(band), band_pairs[band, :, lane], preferred_element_type=F32).astype(BF16)

    for part in range(2):
        rows[part, side] = rows_of(0, part)
    exchange(1, edges_all).wait_recv()
    exchange(2, query_all).wait_recv()
    push_whole.wait_recv()
    rows[0, 1 - side] = rows_of(1, 0)

    scale = math.log2(math.e) / math.sqrt(head)
    span = quad * head
    own_head = iota((quad * nodes, span), 0) // nodes == iota((quad * nodes, span), 1) // head
    tasks = [(step, four) for step in range(chips) for four in range(HEADS // quad)]

    def score(step, four):
        lane = slice(four * span, (four + 1) * span)
        at = slice(step * cap, (step + 1) * cap)
        query = jnp.concatenate([query_all[step][:, lane]] * quad, axis=0)
        query = jnp.where(own_head, query, jnp.zeros_like(query))
        keys_here = jnp.concatenate([rows[0, 0, at, lane], rows[0, 1, at, lane]], axis=0)
        return lax.dot_general(query, keys_here, NT, preferred_element_type=F32)

    def soften(step, scores):
        times = jnp.concatenate([edges_all[step][:, :both].astype(F32)] * quad, axis=0)
        scores = jnp.where(times > 0, scores * scale, -1e30)
        highest = jnp.max(scores, axis=1, keepdims=True)
        raised = jnp.exp2(scores - highest) * times
        return raised.astype(BF16), jnp.broadcast_to(highest, (quad * nodes, 128))

    def blend(step, four, raised):
        lane = slice(four * span, (four + 1) * span)
        at = slice(step * cap, (step + 1) * cap)
        values_here = jnp.concatenate([rows[1, 0, at, lane], rows[1, 1, at, lane]], axis=0)
        mixed = jnp.dot(raised, values_here, preferred_element_type=F32)
        mixed = jnp.where(own_head, mixed, 0.0)
        return functools.reduce(jnp.add, [mixed[j * nodes : (j + 1) * nodes] for j in range(quad)]).astype(BF16)

    stat_lane = iota((lanes, 128), 1)
    board = jnp.zeros((lanes, 128), F32)
    every = jnp.ones((both, 128), BF16)
    scored = [score(step, four) for step, four in tasks]
    rows[1, 1 - side] = rows_of(1, 1)
    softened = [soften(step, one) for (step, four), one in zip(tasks, scored)]
    for (step, four), one in zip(tasks, softened):
        mixes = mix_all if step == 0 else mix_send
        mixes[step, :, four * span : (four + 1) * span] = blend(step, four, one[0])
    for step in range(chips):
        pair = softened[step * (HEADS // quad) : (step + 1) * (HEADS // quad)]
        totals = [jnp.dot(one[0], every, preferred_element_type=F32) for one in pair]
        board = jnp.where(stat_lane == step, jnp.concatenate([one[1] for one in pair], axis=0), board)
        board = jnp.where(stat_lane == chips + step, jnp.concatenate(totals, axis=0), board)
    board = board.T
    for step in range(chips):
        stats = stat_all if step == 0 else stat_send
        stats[step, 0:1, :] = board[step : step + 1]
        stats[step, 1:2, :] = board[chips + step : chips + step + 1]
    for step in others:
        mix_to(step).start()
        stat_to(step).start()

    for step in alike:
        latent_from(step).wait_recv()
        latent_on(step).start()

    loads["wqd"].wait()
    queries_out[...] = (jnp.dot(normed[...], wqd_v[...], preferred_element_type=F32) * scale).astype(BF16)

    loads["wo"].wait()
    loads["dgain"].wait()
    loads["wkvd"].wait()

    exchange(4, stat_all).wait_recv()
    tops = [stat_all[step, 0:1, :] for step in range(chips)]
    sums = [stat_all[step, 1:2, :] for step in range(chips)]
    top = functools.reduce(jnp.maximum, tops)
    shares = [jnp.exp2(one - top) for one in tops]
    whole = functools.reduce(jnp.add, [a * b for a, b in zip(shares, sums)])
    own_node = iota((nodes, lanes), 0) == lax.rem(iota((nodes, lanes), 1), nodes)
    stacked = jnp.concatenate([jnp.where(own_node, share / whole, 0.0) for share in shares], axis=0)
    widen = (iota((lanes, width), 0) // nodes == iota((lanes, width), 1) // head).astype(F32)
    factors = jnp.dot(stacked, widen, precision=HIGH, preferred_element_type=F32).reshape(chips, nodes, width)
    exchange(3, mix_all).wait_recv()
    enc_mixed = jnp.sum(factors * mix_all[...].astype(F32), axis=0).astype(BF16)
    mixes_all[0] = enc_mixed
    for step in others:
        mixes_to(step).start()

    loads["dslot"].wait()
    loads["table"].wait()
    keys = peers * nodes
    dec_cap = table_v.shape[0] * 128 // peers
    slots = dslot_v[...]
    edge_total = slots.shape[0]
    slots = jnp.concatenate([slots] * (8 // edge_total), axis=0)
    columns = []
    for part in range(points // 128):
        piece = slots[:, part * 128 : (part + 1) * 128]
        high = piece // 128
        low = lax.rem(piece, 128)
        need = jnp.zeros_like(piece)
        for line in range(table_v.shape[0]):
            entry = jnp.broadcast_to(table_v[line : line + 1, :], piece.shape)
            need = jnp.where(high == line, jnp.take_along_axis(entry, low, axis=1), need)
        owner = piece // dec_cap
        columns.append(lax.rem(owner, 2) * (chips * nodes) + lax.rem(owner // 2 - here + chips, chips) * nodes + need)
    node = jnp.concatenate(columns, axis=1)
    times = jnp.ones(node.shape, F32)
    for j in range(1, edge_total):
        times = times + jnp.where(node == jnp.concatenate([node[j:], node[:j]], axis=0), 1.0, 0.0)
    node_of[...] = node.astype(F32).T
    worth_of[...] = jnp.log2(times).T
    name = iota((128, keys), 1).astype(F32)

    def bias_block(piece, carry):
        at = pl.ds(pl.multiple_of(piece * 128, 128), 128)
        nodes_here, worth_here = node_of[at, :], worth_of[at, :]
        bias = jnp.full((128, keys), -1e30, F32)
        for j in range(edge_total):
            bias = jnp.where(nodes_here[:, j : j + 1] == name, worth_here[:, j : j + 1], bias)
        bias_out[at, :] = bias
        return carry

    lax.fori_loop(0, points // 128, bias_block, 0)

    latents_beside().wait_recv()
    exchange(5, mixes_all).wait_recv()
    side_nodes = chips * nodes
    update = jnp.dot(mixes_all[...].reshape(side_nodes, width), wo_v[...], preferred_element_type=F32)
    fresh = (latents_all[...].reshape(side_nodes, model).astype(F32) + update).astype(BF16)
    settled = norm_into(fresh, dgain_v[...])
    for number in range(2):
        half = jnp.dot(settled, wkvd_v[:, number * width : (number + 1) * width], preferred_element_type=F32).astype(BF16)
        pairs_mine[number] = half
        pair_over(number).start()
    latent_new[...] = fresh[:nodes]
    near = pl.ds(pl.multiple_of(side * side_nodes, side_nodes), side_nodes)
    over = pl.ds(pl.multiple_of((1 - side) * side_nodes, side_nodes), side_nodes)
    for number in range(2):
        pairs_out[number, near, :] = pairs_mine[number]
    for number in range(2):
        pair_over(number).wait_recv()
        pairs_out[number, over, :] = pairs_in[number]

    for kind, buffer in enumerate((need_all, edges_all, query_all, mix_all, stat_all, mixes_all, latents_all)):
        exchange(kind, buffer).wait_send()
    push_whole.wait_send()
    for number in range(2):
        pair_over(number).wait_send()
    loads["wod"].wait()


BLOCKS = 4


VMEM_LIMIT = 32 * 1024 * 1024


def encode(grid, latent_in, grid_gain, node_gain, dec_gain, w_q_enc, w_kv_enc, w_o_enc, w_q_dec, w_kv_dec, w_o_dec,
           enc_need, enc_slot, enc_count, dec_slot, dec_need):
    peers = lax.axis_size("dom")
    nodes, model = latent_in.shape
    width = w_q_enc.shape[1]
    entries = enc_need.shape[1]
    cap = entries // peers
    points = grid.shape[0]
    chips = peers // 2
    lanes = HEADS * nodes
    far = pl.BlockSpec(memory_space=pltpu.HBM)
    vmem = pl.BlockSpec(memory_space=pltpu.VMEM)
    operands = (grid, latent_in, grid_gain[None], node_gain[None], dec_gain[None], w_q_enc, w_kv_enc, w_o_enc, w_q_dec,
                w_kv_dec, enc_need, enc_slot.T, enc_count[None], dec_slot, dec_need.reshape(-1, 128), w_o_dec)
    return pl.pallas_call(
        functools.partial(encoder_kernel, peers),
        name="encode",
        out_shape=(
            pltpu.VMEM((nodes, model), BF16),
            pltpu.VMEM((2, peers * nodes, width), BF16),
            pltpu.VMEM((points, width), BF16),
            pltpu.VMEM((points, peers * nodes), F32),
            pltpu.VMEM(grid.shape, BF16),
            pltpu.VMEM(w_o_dec.shape, BF16),
        ),
        in_specs=[far] * len(operands),
        out_specs=(vmem,) * 6,
        scratch_shapes=[pltpu.VMEM(one.shape, one.dtype) for one in operands[1:-1]] + [
            pltpu.VMEM((points, model), BF16),
            pltpu.VMEM((2, points, 2 * width), BF16),
            pltpu.VMEM((2, 2, chips * cap, width), BF16),
            pltpu.VMEM((nodes, width), BF16),
            pltpu.VMEM((chips, nodes, 128), BF16),
            pltpu.VMEM((chips, 1, entries), jnp.int32),
            pltpu.VMEM((chips, nodes, width), BF16),
            pltpu.VMEM((chips, nodes, 128), BF16),
            pltpu.VMEM((chips, nodes, model), BF16),
            pltpu.VMEM((chips, nodes, width), BF16),
            pltpu.VMEM((chips, 2, lanes), F32),
            pltpu.VMEM((chips, nodes, width), BF16),
            pltpu.VMEM((chips, 2, lanes), F32),
            pltpu.VMEM((chips, nodes, width), BF16),
            pltpu.VMEM((2, chips * nodes, width), BF16),
            pltpu.VMEM((2, chips * nodes, width), BF16),
            pltpu.VMEM((points, 8), F32),
            pltpu.VMEM((points, 8), F32),
            pltpu.SemaphoreType.DMA((len(operands) - 1 + BLOCKS,)),
            pltpu.SemaphoreType.DMA((7,)),
            pltpu.SemaphoreType.DMA((6 + chips // 2,)),
            pltpu.SemaphoreType.DMA((2,)),
            pltpu.SemaphoreType.DMA((2,)),
            pltpu.SemaphoreType.DMA((2,)),
        ],
        compiler_params=pltpu.CompilerParams(collective_id=0, has_side_effects=True, vmem_limit_bytes=VMEM_LIMIT),
    )(*[pltpu.with_memory_space_constraint(one, pltpu.HBM) for one in operands])


def decoder_kernel(latent_ref, pairs_v, query_v, bias_v, grid_v, wo_v, latent_hbm, out_hbm,
                   out_v, mixed, store_sem):
    points, width = query_v.shape
    head = width // HEADS
    keys = pairs_v.shape[1]
    quad = 4
    chunks = CHUNKS
    tile = points // chunks

    def rows(part):
        return slice(part * tile, (part + 1) * tile)

    stores = [pltpu.make_async_copy(latent_ref, latent_hbm, store_sem.at[chunks * PIECES])]
    stores[0].start()
    lane_head = iota((keys, quad * head), 1) // head
    side_of = iota((keys, 2 * head), 1) // head

    def keys_of(h):
        some = pairs_v[0, :, (h // quad) * quad * head : (h // quad + 1) * quad * head]
        return jnp.where(lane_head == h % quad, some, jnp.zeros_like(some))

    def values_of(pair):
        some = pairs_v[1, :, pair * 2 * head : (pair + 1) * 2 * head]
        none, one = jnp.zeros_like(some), jnp.ones_like(some)
        return jnp.concatenate([
            jnp.concatenate([jnp.where(side_of == side, some, none), jnp.where(side_of == side, one, none)], axis=1)
            for side in range(2)
        ], axis=0)

    for part in range(chunks):
        at = rows(part)
        for pair in range(HEADS // 2):
            four = 2 * pair // quad
            query = query_v[at, four * quad * head : (four + 1) * quad * head]
            raised = []
            for side in range(2):
                scores = lax.dot_general(query, keys_of(2 * pair + side), NT, preferred_element_type=F32)
                scores = scores + bias_v[at, :]
                highest = jnp.max(scores, axis=1, keepdims=True)
                raised.append(jnp.exp2(scores - highest).astype(BF16))
            got = jnp.dot(jnp.concatenate(raised, axis=1), values_of(pair), preferred_element_type=F32)
            mixed[at, pair * 2 * head : (pair + 1) * 2 * head] = (got[:, : 2 * head] / got[:, 2 * head :]).astype(BF16)
        for piece in range(PIECES):
            at = slice(part * tile + piece * (tile // PIECES), part * tile + (piece + 1) * (tile // PIECES))
            update = jnp.dot(mixed[at, :], wo_v[...], preferred_element_type=F32)
            out_v[at, :] = (grid_v[at, :].astype(F32) + update).astype(BF16)
            stores.append(pltpu.make_async_copy(out_v.at[at], out_hbm.at[at], store_sem.at[part * PIECES + piece]))
            stores[-1].start()
    for store in stores:
        store.wait()


CHUNKS = 1
PIECES = 4


def decode(latent_out, pairs, queries, bias, grid, w_o_dec):
    points, model = grid.shape
    width = queries.shape[1]
    vmem = pl.BlockSpec(memory_space=pltpu.VMEM)
    far = pl.BlockSpec(memory_space=pltpu.HBM)
    return pl.pallas_call(
        decoder_kernel,
        name="decode",
        out_shape=(
            jax.ShapeDtypeStruct(latent_out.shape, BF16),
            jax.ShapeDtypeStruct(grid.shape, BF16),
        ),
        in_specs=[vmem] * 6,
        out_specs=(far, far),
        scratch_shapes=[
            pltpu.VMEM(grid.shape, BF16),
            pltpu.VMEM((points, width), BF16),
            pltpu.SemaphoreType.DMA((CHUNKS * PIECES + 1,)),
        ],
        compiler_params=pltpu.CompilerParams(vmem_limit_bytes=VMEM_LIMIT),
    )(latent_out, pairs, queries, bias, grid, w_o_dec)


def by_kernels(grid, latent_in, grid_gain, node_gain, dec_gain, w_q_enc, w_kv_enc, w_o_enc,
               w_q_dec, w_kv_dec, w_o_dec, enc_need, enc_slot, enc_count, dec_need, dec_slot):
    return decode(*encode(
        grid, latent_in, grid_gain, node_gain, dec_gain, w_q_enc, w_kv_enc, w_o_enc, w_q_dec, w_kv_dec, w_o_dec,
        enc_need, enc_slot, enc_count, dec_slot, dec_need))


def chosen_form(*args):
    grid, latent_in, enc_need, dec_slot = args[0], args[1], args[11], args[15]
    peers = lax.axis_size("dom")
    cap = enc_need.shape[1] // peers
    small = latent_in.shape[0] * peers <= 256
    fits = peers % 4 == 0 and 128 % cap == 0 and cap in (32, 64) and peers <= 128 and HEADS * latent_in.shape[0] == 128 and grid.shape[0] % 512 == 0
    if small and fits and 8 % dec_slot.shape[0] == 0:
        return by_kernels(*args)
    return on_device(*args)


def solution(mesh):
    both, rep = P(("groups", "dom"), None), P()
    return jax.shard_map(
        chosen_form,
        mesh=mesh,
        in_specs=(both, both, *([rep] * 9), P("dom", None), P(None, "dom"), P("dom"), P("dom", None), P(None, "dom")),
        out_specs=(both, both),
        check_vma=False,
    )
```

```python
import functools
import math

import jax
import jax.numpy as jnp
from jax import lax
from jax.experimental import pallas as pl
from jax.experimental.pallas import tpu as pltpu
from jax.sharding import PartitionSpec as P

HEADS = 8
norm_eps = 1e-06
F32 = jnp.float32
BF16 = jnp.bfloat16


def rms_norm(values, weight_gain):
    widened = values.astype(F32)
    spread = jnp.mean(widened * widened, axis=-1, keepdims=True)
    return (widened * lax.rsqrt(spread + norm_eps) * weight_gain).astype(BF16)


def attend_dense(queries, pairs, edges):
    rows, width = queries.shape
    head = width // HEADS
    q = queries.reshape(rows, HEADS, head)
    k = pairs[:, :width].reshape(-1, HEADS, head)
    v = pairs[:, width:].reshape(-1, HEADS, head)
    scores = jnp.einsum("rhd,khd->hrk", q, k, preferred_element_type=F32)
    scores = jnp.where(edges[None] > 0, scores * (1.0 / math.sqrt(head)), -1e30)
    highest = jnp.max(scores, axis=-1, keepdims=True)
    raised = jnp.exp(scores - highest) * edges[None]
    weights = (raised / jnp.sum(raised, axis=-1, keepdims=True)).astype(BF16)
    mixed = jnp.einsum("hrk,khd->rhd", weights, v, preferred_element_type=F32)
    return mixed.reshape(rows, width).astype(BF16)


def on_device(grid, latent_in, grid_gain, node_gain, dec_gain, w_q_enc, w_kv_enc, w_o_enc,
              w_q_dec, w_kv_dec, w_o_dec, enc_need, enc_slot, enc_count, dec_need, dec_slot):
    peers = lax.axis_size("dom")
    nodes = latent_in.shape[0]
    normed_grid = rms_norm(grid, grid_gain)
    wanted = lax.all_to_all(enc_need.reshape(peers, -1), "dom", split_axis=0, concat_axis=0, tiled=True)
    band = jnp.arange(grid.shape[0], dtype=jnp.int32)
    pick = (wanted.reshape(-1)[:, None] == band[None, :]).astype(BF16)
    chosen = jnp.dot(pick, normed_grid, preferred_element_type=F32).astype(BF16)
    rows = jnp.dot(chosen, w_kv_enc, preferred_element_type=F32).astype(BF16)
    arrived = lax.all_to_all(rows, "dom", split_axis=0, concat_axis=0, tiled=True)
    enc_queries = jnp.dot(rms_norm(latent_in, node_gain), w_q_enc, preferred_element_type=F32).astype(BF16)
    live = jnp.arange(enc_slot.shape[0], dtype=jnp.int32)[:, None] < enc_count[None, :]
    slot_row = jnp.arange(enc_need.shape[1], dtype=jnp.int32)
    enc_edges = jnp.sum((live[:, :, None] & (enc_slot[:, :, None] == slot_row)).astype(F32), axis=0)
    enc_mixed = attend_dense(enc_queries, arrived, enc_edges)
    enc_update = jnp.dot(enc_mixed, w_o_enc, preferred_element_type=F32)
    latent_out = (latent_in.astype(F32) + enc_update).astype(BF16)
    latent_pairs = jnp.dot(rms_norm(latent_out, dec_gain), w_kv_dec, preferred_element_type=F32).astype(BF16)
    dec_queries = jnp.dot(normed_grid, w_q_dec, preferred_element_type=F32).astype(BF16)
    everyone = lax.all_gather(latent_pairs, "dom", axis=0, tiled=True)
    total = dec_need.shape[1]
    cap = total // peers
    lanes = 128
    table = dec_need.reshape(total // lanes, lanes).astype(BF16)
    high = (dec_slot // lanes)[:, :, None] == jnp.arange(total // lanes, dtype=jnp.int32)
    low = (dec_slot % lanes)[:, :, None] == jnp.arange(lanes, dtype=jnp.int32)
    need = jnp.einsum("jgt,tl->jgl", high.astype(BF16), table, preferred_element_type=F32)
    need = jnp.sum(jnp.where(low, need, 0.0), axis=-1).astype(jnp.int32)
    node = (dec_slot // cap) * nodes + need
    dec_edges = jnp.sum((node[:, :, None] == jnp.arange(peers * nodes, dtype=jnp.int32)).astype(F32), axis=0)
    dec_mixed = attend_dense(dec_queries, everyone, dec_edges)
    dec_update = jnp.dot(dec_mixed, w_o_dec, preferred_element_type=F32)
    grid_out = (grid.astype(F32) + dec_update).astype(BF16)
    return (latent_out, grid_out)


NT = (((1,), (1,)), ((), ()))
TN = (((0,), (0,)), ((), ()))
HIGH = lax.Precision.HIGHEST


def iota(shape, dim):
    return lax.broadcasted_iota(jnp.int32, shape, dim)


def norm_into(values, gain):
    widened = values.astype(F32)
    spread = jnp.mean(widened * widened, axis=-1, keepdims=True)
    return (widened * lax.rsqrt(spread + norm_eps) * gain).astype(BF16)


def encoder_kernel(
    peers, grid_hbm, latent_hbm, ggain_hbm, ngain_hbm, dgain_hbm, wq_hbm, wkv_hbm, wo_hbm, wqd_hbm, wkvd_hbm,
    need_hbm, slot_hbm, count_hbm, dslot_hbm, table_hbm, wod_hbm,
    latent_new, pairs_out, queries_out, bias_out, grid_v, wod_v,
    latent_v, ggain_v, ngain_v, dgain_v, wq_v, wkv_v, wo_v, wqd_v, wkvd_v, need_v, slot_v, count_v, dslot_v,
    table_v, normed, band_pairs, rows, query_mine, edges_mine,
    need_all, query_all, edges_all, latents_all, mix_send, stat_send, mix_all, stat_all, mixes_all, pairs_mine, pairs_in,
    node_of, worth_of, load_sem, send_sem, recv_sem, push_sem, pair_send, pair_recv,
):
    me = lax.axis_index("dom")
    nodes, model = latent_v.shape
    width = wq_v.shape[1]
    head = width // HEADS
    cap = need_v.shape[1] // peers
    group = 128 // cap
    chips = peers // 2
    side = lax.rem(me, 2)
    partner = me + 1 - 2 * side
    points = grid_v.shape[0]
    lanes = HEADS * nodes
    both = 2 * cap
    quad = 4
    here = me // 2
    beside = here + 1 - 2 * lax.rem(here, 2)
    blocks = BLOCKS
    block = points // blocks

    barrier = pltpu.get_barrier_semaphore()
    for to in [lax.rem(me + 2 * step, peers) for step in range(1, chips)] + [partner]:
        pl.semaphore_signal(barrier, inc=1, device_id={"dom": to}, device_id_type=pl.DeviceIdType.MESH)

    def block_at(number):
        return slice(number * block, (number + 1) * block)

    pairs_of_refs = {
        "slot": (slot_hbm, slot_v), "count": (count_hbm, count_v), "need": (need_hbm, need_v),
        "latent": (latent_hbm, latent_v), "ngain": (ngain_hbm, ngain_v), "wq": (wq_hbm, wq_v),
        "ggain": (ggain_hbm, ggain_v),
    }
    for number in range(blocks):
        pairs_of_refs[number] = (grid_hbm.at[block_at(number)], grid_v.at[block_at(number)])
    pairs_of_refs.update({
        "wkv": (wkv_hbm, wkv_v), "wqd": (wqd_hbm, wqd_v), "dslot": (dslot_hbm, dslot_v), "table": (table_hbm, table_v),
        "wo": (wo_hbm, wo_v), "dgain": (dgain_hbm, dgain_v), "wkvd": (wkvd_hbm, wkvd_v), "wod": (wod_hbm, wod_v),
    })
    loads = {}
    for number, (name, (source, target)) in enumerate(pairs_of_refs.items()):
        loads[name] = pltpu.make_async_copy(source, target, load_sem.at[number])
        loads[name].start()

    def message(kind, source, target, to, landing=None):
        return pltpu.make_async_remote_copy(
            src_ref=source,
            dst_ref=target,
            send_sem=send_sem.at[kind],
            recv_sem=recv_sem.at[kind if landing is None else landing],
            device_id={"dom": to},
            device_id_type=pl.DeviceIdType.MESH,
        )

    def chip(step):
        return lax.rem(me + 2 * step, peers)

    def place(step):
        return lax.rem(here + step, chips)

    def exchange(kind, buffer):
        rest = buffer.at[pl.ds(1, chips - 1)]
        return message(kind, rest, rest, partner)

    def need_to(step):
        return message(0, need_v, need_all.at[chips - step], chip(step))

    def edges_to(step):
        return message(1, edges_mine.at[place(step)], edges_all.at[chips - step], chip(step))

    def query_to(step):
        return message(2, query_mine, query_all.at[chips - step], chip(step))

    def mix_to(step):
        return message(3, mix_send.at[step], mix_all.at[chips - step], chip(step))

    def stat_to(step):
        return message(4, stat_send.at[step], stat_all.at[chips - step], chip(step))

    def mixes_to(step):
        return message(5, mixes_all.at[0], mixes_all.at[chips - step], chip(step))

    apart = chips + here - beside

    def latent_to(step, slot):
        return message(6, latents_all.at[0], latents_all.at[slot], chip(step), 6 + slot // 2)

    def latent_from(slot):
        return message(6, latents_all.at[slot], latents_all.at[slot], partner, 6 + slot // 2)

    def latent_on(slot):
        return message(
            6, latents_all.at[slot], latents_all.at[lax.rem(slot + apart, chips)], 2 * beside + side, 6
        )

    def latents_beside():
        some = latents_all.at[pl.ds(0, chips // 2)]
        return message(6, some, some, partner, 6)

    push_whole = pltpu.make_async_remote_copy(
        src_ref=band_pairs.at[0],
        dst_ref=band_pairs.at[1],
        send_sem=push_sem.at[0],
        recv_sem=push_sem.at[1],
        device_id={"dom": partner},
        device_id_type=pl.DeviceIdType.MESH,
    )

    def pair_over(number):
        return pltpu.make_async_remote_copy(
            src_ref=pairs_mine.at[number],
            dst_ref=pairs_in.at[number],
            send_sem=pair_send.at[number],
            recv_sem=pair_recv.at[number],
            device_id={"dom": partner},
            device_id_type=pl.DeviceIdType.MESH,
        )

    def push(number):
        return pltpu.make_async_remote_copy(
            src_ref=band_pairs.at[0, block_at(number)],
            dst_ref=band_pairs.at[1, block_at(number)],
            send_sem=push_sem.at[0],
            recv_sem=push_sem.at[1],
            device_id={"dom": partner},
            device_id_type=pl.DeviceIdType.MESH,
        )

    others = [step for low in range(1, chips // 2) for step in (low, chips - low)] + [chips // 2]
    alike = range(2, chips, 2)

    loads["slot"].wait()
    loads["count"].wait()
    edge_total = slot_v.shape[1]
    own = iota((nodes, nodes), 0) == iota((nodes, nodes), 1)
    counts = jnp.sum(jnp.where(own, count_v[...].astype(F32), 0.0), axis=1, keepdims=True)
    slots = jnp.where(iota(slot_v.shape, 1).astype(F32) < counts, slot_v[...], -1)
    entry = iota((nodes, peers * cap), 1)
    tally = jnp.zeros((nodes, peers * cap), F32)
    for j in range(edge_total):
        tally = tally + jnp.where(slots[:, j : j + 1] == entry, 1.0, 0.0)
    tally = tally.astype(BF16)
    for number in range(chips):
        own_part = tally[:, number * both : (number + 1) * both]
        edges_mine[number] = jnp.concatenate([own_part] * (128 // both), axis=1)
    edges_all[0] = edges_mine[here]
    loads["need"].wait()
    need_all[0] = need_v[...]
    loads["latent"].wait()
    loads["ngain"].wait()
    loads["wq"].wait()
    queries = jnp.dot(
        norm_into(latent_v[...], ngain_v[...]), wq_v[...], preferred_element_type=F32
    ).astype(BF16)
    query_mine[...] = queries
    query_all[0] = queries
    latents_all[0] = latent_v[...]

    pl.semaphore_wait(barrier, chips)
    for step in others:
        need_to(step).start()
    for step in others:
        edges_to(step).start()
        query_to(step).start()

    loads["ggain"].wait()
    for number in range(blocks):
        loads[number].wait()
    loads["wkv"].wait()
    settled = norm_into(grid_v[block_at(0), :], ggain_v[...])
    for number in range(blocks):
        at = block_at(number)
        normed[at, :] = settled
        band_pairs[0, at, :] = jnp.dot(settled, wkv_v[...], preferred_element_type=F32).astype(BF16)
        if number + 1 < blocks:
            settled = norm_into(grid_v[block_at(number + 1), :], ggain_v[...])
        push(number).start()
    for step in alike:
        latent_to(step, chips - step).start()
    latent_on(0).start()

    exchange(0, need_all).wait_recv()
    base = pl.multiple_of((me // group) * 128, 128)
    lists = need_all[:, :, pl.ds(base, 128)]
    within = lax.rem(me // 2, group // 2) * both
    asked = jnp.broadcast_to(lists, (chips, cap, 128)).astype(F32)
    spot = iota((chips, cap, 128), 1)
    lane = iota((chips, cap, 128), 2)
    wanted = []
    for band in (side, 1 - side):
        picked = jnp.where(lane == within + band * cap + spot, asked, 0.0)
        wanted.append(jnp.sum(picked, axis=2, keepdims=True).astype(jnp.int32).reshape(chips * cap, 1))
    point = iota((chips * cap, points), 1)
    def pick_of(band):
        return jnp.where(wanted[band] == point, 1.0, 0.0).astype(BF16)

    def rows_of(band, part):
        lane = slice(part * width, (part + 1) * width)
        return jnp.dot(pick_of(band), band_pairs[band, :, lane], preferred_element_type=F32).astype(BF16)

    for part in range(2):
        rows[part, side] = rows_of(0, part)
    exchange(1, edges_all).wait_recv()
    exchange(2, query_all).wait_recv()
    push_whole.wait_recv()
    rows[0, 1 - side] = rows_of(1, 0)

    scale = math.log2(math.e) / math.sqrt(head)
    span = quad * head
    own_head = iota((quad * nodes, span), 0) // nodes == iota((quad * nodes, span), 1) // head
    tasks = [(step, four) for step in range(chips) for four in range(HEADS // quad)]

    def score(step, four):
        lane = slice(four * span, (four + 1) * span)
        at = slice(step * cap, (step + 1) * cap)
        query = jnp.concatenate([query_all[step][:, lane]] * quad, axis=0)
        query = jnp.where(own_head, query, jnp.zeros_like(query))
        keys_here = jnp.concatenate([rows[0, 0, at, lane], rows[0, 1, at, lane]], axis=0)
        return lax.dot_general(query, keys_here, NT, preferred_element_type=F32)

    def soften(step, scores):
        times = jnp.concatenate([edges_all[step][:, :both].astype(F32)] * quad, axis=0)
        scores = jnp.where(times > 0, scores * scale, -1e30)
        highest = jnp.max(scores, axis=1, keepdims=True)
        raised = jnp.exp2(scores - highest) * times
        return raised.astype(BF16), jnp.broadcast_to(highest, (quad * nodes, 128))

    def blend(step, four, raised):
        lane = slice(four * span, (four + 1) * span)
        at = slice(step * cap, (step + 1) * cap)
        values_here = jnp.concatenate([rows[1, 0, at, lane], rows[1, 1, at, lane]], axis=0)
        mixed = jnp.dot(raised, values_here, preferred_element_type=F32)
        mixed = jnp.where(own_head, mixed, 0.0)
        return functools.reduce(jnp.add, [mixed[j * nodes : (j + 1) * nodes] for j in range(quad)]).astype(BF16)

    stat_lane = iota((lanes, 128), 1)
    board = jnp.zeros((lanes, 128), F32)
    every = jnp.ones((both, 128), BF16)
    scored = [score(step, four) for step, four in tasks]
    rows[1, 1 - side] = rows_of(1, 1)
    softened = [soften(step, one) for (step, four), one in zip(tasks, scored)]
    for (step, four), one in zip(tasks, softened):
        mixes = mix_all if step == 0 else mix_send
        mixes[step, :, four * span : (four + 1) * span] = blend(step, four, one[0])
    for step in range(chips):
        pair = softened[step * (HEADS // quad) : (step + 1) * (HEADS // quad)]
        totals = [jnp.dot(one[0], every, preferred_element_type=F32) for one in pair]
        board = jnp.where(stat_lane == step, jnp.concatenate([one[1] for one in pair], axis=0), board)
        board = jnp.where(stat_lane == chips + step, jnp.concatenate(totals, axis=0), board)
    board = board.T
    for step in range(chips):
        stats = stat_all if step == 0 else stat_send
        stats[step, 0:1, :] = board[step : step + 1]
        stats[step, 1:2, :] = board[chips + step : chips + step + 1]
    for step in others:
        mix_to(step).start()
        stat_to(step).start()

    for step in alike:
        latent_from(step).wait_recv()
        latent_on(step).start()

    loads["wqd"].wait()
    queries_out[...] = (jnp.dot(normed[...], wqd_v[...], preferred_element_type=F32) * scale).astype(BF16)

    loads["wo"].wait()
    loads["dgain"].wait()
    loads["wkvd"].wait()

    exchange(4, stat_all).wait_recv()
    tops = [stat_all[step, 0:1, :] for step in range(chips)]
    sums = [stat_all[step, 1:2, :] for step in range(chips)]
    top = functools.reduce(jnp.maximum, tops)
    shares = [jnp.exp2(one - top) for one in tops]
    whole = functools.reduce(jnp.add, [a * b for a, b in zip(shares, sums)])
    own_node = iota((nodes, lanes), 0) == lax.rem(iota((nodes, lanes), 1), nodes)
    stacked = jnp.concatenate([jnp.where(own_node, share / whole, 0.0) for share in shares], axis=0)
    widen = (iota((lanes, width), 0) // nodes == iota((lanes, width), 1) // head).astype(F32)
    factors = jnp.dot(stacked, widen, precision=HIGH, preferred_element_type=F32).reshape(chips, nodes, width)
    exchange(3, mix_all).wait_recv()
    enc_mixed = jnp.sum(factors * mix_all[...].astype(F32), axis=0).astype(BF16)
    mixes_all[0] = enc_mixed
    for step in others:
        mixes_to(step).start()

    loads["dslot"].wait()
    loads["table"].wait()
    keys = peers * nodes
    dec_cap = table_v.shape[0] * 128 // peers
    slots = dslot_v[...]
    edge_total = slots.shape[0]
    slots = jnp.concatenate([slots] * (8 // edge_total), axis=0)
    columns = []
    for part in range(points // 128):
        piece = slots[:, part * 128 : (part + 1) * 128]
        high = piece // 128
        low = lax.rem(piece, 128)
        need = jnp.zeros_like(piece)
        for line in range(table_v.shape[0]):
            entry = jnp.broadcast_to(table_v[line : line + 1, :], piece.shape)
            need = jnp.where(high == line, jnp.take_along_axis(entry, low, axis=1), need)
        owner = piece // dec_cap
        columns.append(lax.rem(owner, 2) * (chips * nodes) + lax.rem(owner // 2 - here + chips, chips) * nodes + need)
    node = jnp.concatenate(columns, axis=1)
    times = jnp.ones(node.shape, F32)
    for j in range(1, edge_total):
        times = times + jnp.where(node == jnp.concatenate([node[j:], node[:j]], axis=0), 1.0, 0.0)
    node_of[...] = node.astype(F32).T
    worth_of[...] = jnp.log2(times).T
    name = iota((128, keys), 1).astype(F32)

    def bias_block(piece, carry):
        at = pl.ds(pl.multiple_of(piece * 128, 128), 128)
        nodes_here, worth_here = node_of[at, :], worth_of[at, :]
        bias = jnp.full((128, keys), -1e30, F32)
        for j in range(edge_total):
            bias = jnp.where(nodes_here[:, j : j + 1] == name, worth_here[:, j : j + 1], bias)
        bias_out[at, :] = bias
        return carry

    lax.fori_loop(0, points // 128, bias_block, 0)

    latents_beside().wait_recv()
    exchange(5, mixes_all).wait_recv()
    side_nodes = chips * nodes
    update = jnp.dot(mixes_all[...].reshape(side_nodes, width), wo_v[...], preferred_element_type=F32)
    fresh = (latents_all[...].reshape(side_nodes, model).astype(F32) + update).astype(BF16)
    settled = norm_into(fresh, dgain_v[...])
    for number in range(2):
        half = jnp.dot(settled, wkvd_v[:, number * width : (number + 1) * width], preferred_element_type=F32).astype(BF16)
        pairs_mine[number] = half
        pair_over(number).start()
    latent_new[...] = fresh[:nodes]
    near = pl.ds(pl.multiple_of(side * side_nodes, side_nodes), side_nodes)
    over = pl.ds(pl.multiple_of((1 - side) * side_nodes, side_nodes), side_nodes)
    for number in range(2):
        pairs_out[number, near, :] = pairs_mine[number]
    for number in range(2):
        pair_over(number).wait_recv()
        pairs_out[number, over, :] = pairs_in[number]

    for kind, buffer in enumerate((need_all, edges_all, query_all, mix_all, stat_all, mixes_all, latents_all)):
        exchange(kind, buffer).wait_send()
    push_whole.wait_send()
    for number in range(2):
        pair_over(number).wait_send()
    loads["wod"].wait()


BLOCKS = 4


VMEM_LIMIT = 32 * 1024 * 1024


def encode(grid, latent_in, grid_gain, node_gain, dec_gain, w_q_enc, w_kv_enc, w_o_enc, w_q_dec, w_kv_dec, w_o_dec,
           enc_need, enc_slot, enc_count, dec_slot, dec_need):
    peers = lax.axis_size("dom")
    nodes, model = latent_in.shape
    width = w_q_enc.shape[1]
    entries = enc_need.shape[1]
    cap = entries // peers
    points = grid.shape[0]
    chips = peers // 2
    lanes = HEADS * nodes
    far = pl.BlockSpec(memory_space=pltpu.HBM)
    vmem = pl.BlockSpec(memory_space=pltpu.VMEM)
    operands = (grid, latent_in, grid_gain[None], node_gain[None], dec_gain[None], w_q_enc, w_kv_enc, w_o_enc, w_q_dec,
                w_kv_dec, enc_need, enc_slot.T, enc_count[None], dec_slot, dec_need.reshape(-1, 128), w_o_dec)
    return pl.pallas_call(
        functools.partial(encoder_kernel, peers),
        name="encode",
        out_shape=(
            pltpu.VMEM((nodes, model), BF16),
            pltpu.VMEM((2, peers * nodes, width), BF16),
            pltpu.VMEM((points, width), BF16),
            pltpu.VMEM((points, peers * nodes), F32),
            pltpu.VMEM(grid.shape, BF16),
            pltpu.VMEM(w_o_dec.shape, BF16),
        ),
        in_specs=[far] * len(operands),
        out_specs=(vmem,) * 6,
        scratch_shapes=[pltpu.VMEM(one.shape, one.dtype) for one in operands[1:-1]] + [
            pltpu.VMEM((points, model), BF16),
            pltpu.VMEM((2, points, 2 * width), BF16),
            pltpu.VMEM((2, 2, chips * cap, width), BF16),
            pltpu.VMEM((nodes, width), BF16),
            pltpu.VMEM((chips, nodes, 128), BF16),
            pltpu.VMEM((chips, 1, entries), jnp.int32),
            pltpu.VMEM((chips, nodes, width), BF16),
            pltpu.VMEM((chips, nodes, 128), BF16),
            pltpu.VMEM((chips, nodes, model), BF16),
            pltpu.VMEM((chips, nodes, width), BF16),
            pltpu.VMEM((chips, 2, lanes), F32),
            pltpu.VMEM((chips, nodes, width), BF16),
            pltpu.VMEM((chips, 2, lanes), F32),
            pltpu.VMEM((chips, nodes, width), BF16),
            pltpu.VMEM((2, chips * nodes, width), BF16),
            pltpu.VMEM((2, chips * nodes, width), BF16),
            pltpu.VMEM((points, 8), F32),
            pltpu.VMEM((points, 8), F32),
            pltpu.SemaphoreType.DMA((len(operands) - 1 + BLOCKS,)),
            pltpu.SemaphoreType.DMA((7,)),
            pltpu.SemaphoreType.DMA((6 + chips // 2,)),
            pltpu.SemaphoreType.DMA((2,)),
            pltpu.SemaphoreType.DMA((2,)),
            pltpu.SemaphoreType.DMA((2,)),
        ],
        compiler_params=pltpu.CompilerParams(collective_id=0, has_side_effects=True, vmem_limit_bytes=VMEM_LIMIT),
    )(*[pltpu.with_memory_space_constraint(one, pltpu.HBM) for one in operands])


def decoder_kernel(latent_ref, pairs_v, query_v, bias_v, grid_v, wo_v, latent_hbm, out_hbm,
                   out_v, mixed, store_sem):
    points, width = query_v.shape
    head = width // HEADS
    keys = pairs_v.shape[1]
    quad = 4

    def rows(part, size):
        return slice(part * size, (part + 1) * size)

    stores = [pltpu.make_async_copy(latent_ref, latent_hbm, store_sem.at[PIECES])]
    stores[0].start()
    lane_head = iota((keys, quad * head), 1) // head
    side_of = iota((keys, 2 * head), 1) // head

    def keys_of(h):
        some = pairs_v[0, :, (h // quad) * quad * head : (h // quad + 1) * quad * head]
        return jnp.where(lane_head == h % quad, some, jnp.zeros_like(some))

    def values_of(pair):
        some = pairs_v[1, :, pair * 2 * head : (pair + 1) * 2 * head]
        none, one = jnp.zeros_like(some), jnp.ones_like(some)
        return jnp.concatenate([
            jnp.concatenate([jnp.where(side_of == side, some, none), jnp.where(side_of == side, one, none)], axis=1)
            for side in range(2)
        ], axis=0)

    def attend(pair, at):
        four = 2 * pair // quad
        query = query_v[at, four * quad * head : (four + 1) * quad * head]
        raised = []
        for side in range(2):
            scores = lax.dot_general(query, keys_of(2 * pair + side), NT, preferred_element_type=F32)
            scores = scores + bias_v[at, :]
            highest = jnp.max(scores, axis=1, keepdims=True)
            raised.append(jnp.exp2(scores - highest).astype(BF16))
        got = jnp.dot(jnp.concatenate(raised, axis=1), values_of(pair), preferred_element_type=F32)
        mixed[at, pair * 2 * head : (pair + 1) * 2 * head] = (got[:, : 2 * head] / got[:, 2 * head :]).astype(BF16)

    def project(number, size):
        at = slice(number * size, (number + 1) * size)
        update = jnp.dot(mixed[at, :], wo_v[...], preferred_element_type=F32)
        out_v[at, :] = (grid_v[at, :].astype(F32) + update).astype(BF16)

    def leave(number, size):
        at = slice(number * size, (number + 1) * size)
        stores.append(pltpu.make_async_copy(out_v.at[at], out_hbm.at[at], store_sem.at[number]))
        stores[-1].start()

    for pair in range(HEADS // 2):
        for part in range(2):
            attend(pair, rows(part, points // 2))
    for number in range(PIECES):
        project(number, points // PIECES)
        leave(number, points // PIECES)
    for store in stores:
        store.wait()


PIECES = 8


def decode(latent_out, pairs, queries, bias, grid, w_o_dec):
    points, model = grid.shape
    width = queries.shape[1]
    vmem = pl.BlockSpec(memory_space=pltpu.VMEM)
    far = pl.BlockSpec(memory_space=pltpu.HBM)
    return pl.pallas_call(
        decoder_kernel,
        name="decode",
        out_shape=(
            jax.ShapeDtypeStruct(latent_out.shape, BF16),
            jax.ShapeDtypeStruct(grid.shape, BF16),
        ),
        in_specs=[vmem] * 6,
        out_specs=(far, far),
        scratch_shapes=[
            pltpu.VMEM(grid.shape, BF16),
            pltpu.VMEM((points, width), BF16),
            pltpu.SemaphoreType.DMA((PIECES + 1,)),
        ],
        compiler_params=pltpu.CompilerParams(vmem_limit_bytes=VMEM_LIMIT),
    )(latent_out, pairs, queries, bias, grid, w_o_dec)


def by_kernels(grid, latent_in, grid_gain, node_gain, dec_gain, w_q_enc, w_kv_enc, w_o_enc,
               w_q_dec, w_kv_dec, w_o_dec, enc_need, enc_slot, enc_count, dec_need, dec_slot):
    return decode(*encode(
        grid, latent_in, grid_gain, node_gain, dec_gain, w_q_enc, w_kv_enc, w_o_enc, w_q_dec, w_kv_dec, w_o_dec,
        enc_need, enc_slot, enc_count, dec_slot, dec_need))


def chosen_form(*args):
    grid, latent_in, enc_need, dec_slot = args[0], args[1], args[11], args[15]
    peers = lax.axis_size("dom")
    cap = enc_need.shape[1] // peers
    small = latent_in.shape[0] * peers <= 256
    fits = peers % 4 == 0 and 128 % cap == 0 and cap in (32, 64) and peers <= 128 and HEADS * latent_in.shape[0] == 128 and grid.shape[0] % 512 == 0
    if small and fits and 8 % dec_slot.shape[0] == 0:
        return by_kernels(*args)
    return on_device(*args)


def solution(mesh):
    both, rep = P(("groups", "dom"), None), P()
    return jax.shard_map(
        chosen_form,
        mesh=mesh,
        in_specs=(both, both, *([rep] * 9), P("dom", None), P(None, "dom"), P("dom"), P("dom", None), P(None, "dom")),
        out_specs=(both, both),
        check_vma=False,
    )
```

```python
import functools
import math

import jax
import jax.numpy as jnp
from jax import lax
from jax.experimental import pallas as pl
from jax.experimental.pallas import tpu as pltpu
from jax.sharding import PartitionSpec as P

HEADS = 8
norm_eps = 1e-06
F32 = jnp.float32
BF16 = jnp.bfloat16


def rms_norm(values, weight_gain):
    widened = values.astype(F32)
    spread = jnp.mean(widened * widened, axis=-1, keepdims=True)
    return (widened * lax.rsqrt(spread + norm_eps) * weight_gain).astype(BF16)


def attend_dense(queries, pairs, edges):
    rows, width = queries.shape
    head = width // HEADS
    q = queries.reshape(rows, HEADS, head)
    k = pairs[:, :width].reshape(-1, HEADS, head)
    v = pairs[:, width:].reshape(-1, HEADS, head)
    scores = jnp.einsum("rhd,khd->hrk", q, k, preferred_element_type=F32)
    scores = jnp.where(edges[None] > 0, scores * (1.0 / math.sqrt(head)), -1e30)
    highest = jnp.max(scores, axis=-1, keepdims=True)
    raised = jnp.exp(scores - highest) * edges[None]
    weights = (raised / jnp.sum(raised, axis=-1, keepdims=True)).astype(BF16)
    mixed = jnp.einsum("hrk,khd->rhd", weights, v, preferred_element_type=F32)
    return mixed.reshape(rows, width).astype(BF16)


def on_device(grid, latent_in, grid_gain, node_gain, dec_gain, w_q_enc, w_kv_enc, w_o_enc,
              w_q_dec, w_kv_dec, w_o_dec, enc_need, enc_slot, enc_count, dec_need, dec_slot):
    peers = lax.axis_size("dom")
    nodes = latent_in.shape[0]
    normed_grid = rms_norm(grid, grid_gain)
    wanted = lax.all_to_all(enc_need.reshape(peers, -1), "dom", split_axis=0, concat_axis=0, tiled=True)
    band = jnp.arange(grid.shape[0], dtype=jnp.int32)
    pick = (wanted.reshape(-1)[:, None] == band[None, :]).astype(BF16)
    chosen = jnp.dot(pick, normed_grid, preferred_element_type=F32).astype(BF16)
    rows = jnp.dot(chosen, w_kv_enc, preferred_element_type=F32).astype(BF16)
    arrived = lax.all_to_all(rows, "dom", split_axis=0, concat_axis=0, tiled=True)
    enc_queries = jnp.dot(rms_norm(latent_in, node_gain), w_q_enc, preferred_element_type=F32).astype(BF16)
    live = jnp.arange(enc_slot.shape[0], dtype=jnp.int32)[:, None] < enc_count[None, :]
    slot_row = jnp.arange(enc_need.shape[1], dtype=jnp.int32)
    enc_edges = jnp.sum((live[:, :, None] & (enc_slot[:, :, None] == slot_row)).astype(F32), axis=0)
    enc_mixed = attend_dense(enc_queries, arrived, enc_edges)
    enc_update = jnp.dot(enc_mixed, w_o_enc, preferred_element_type=F32)
    latent_out = (latent_in.astype(F32) + enc_update).astype(BF16)
    latent_pairs = jnp.dot(rms_norm(latent_out, dec_gain), w_kv_dec, preferred_element_type=F32).astype(BF16)
    dec_queries = jnp.dot(normed_grid, w_q_dec, preferred_element_type=F32).astype(BF16)
    everyone = lax.all_gather(latent_pairs, "dom", axis=0, tiled=True)
    total = dec_need.shape[1]
    cap = total // peers
    lanes = 128
    table = dec_need.reshape(total // lanes, lanes).astype(BF16)
    high = (dec_slot // lanes)[:, :, None] == jnp.arange(total // lanes, dtype=jnp.int32)
    low = (dec_slot % lanes)[:, :, None] == jnp.arange(lanes, dtype=jnp.int32)
    need = jnp.einsum("jgt,tl->jgl", high.astype(BF16), table, preferred_element_type=F32)
    need = jnp.sum(jnp.where(low, need, 0.0), axis=-1).astype(jnp.int32)
    node = (dec_slot // cap) * nodes + need
    dec_edges = jnp.sum((node[:, :, None] == jnp.arange(peers * nodes, dtype=jnp.int32)).astype(F32), axis=0)
    dec_mixed = attend_dense(dec_queries, everyone, dec_edges)
    dec_update = jnp.dot(dec_mixed, w_o_dec, preferred_element_type=F32)
    grid_out = (grid.astype(F32) + dec_update).astype(BF16)
    return (latent_out, grid_out)


NT = (((1,), (1,)), ((), ()))
TN = (((0,), (0,)), ((), ()))
HIGH = lax.Precision.HIGHEST


def iota(shape, dim):
    return lax.broadcasted_iota(jnp.int32, shape, dim)


def norm_into(values, gain):
    widened = values.astype(F32)
    spread = jnp.mean(widened * widened, axis=-1, keepdims=True)
    return (widened * lax.rsqrt(spread + norm_eps) * gain).astype(BF16)


def encoder_kernel(
    peers, grid_hbm, latent_hbm, ggain_hbm, ngain_hbm, dgain_hbm, wq_hbm, wkv_hbm, wo_hbm, wqd_hbm, wkvd_hbm,
    need_hbm, slot_hbm, count_hbm, dslot_hbm, table_hbm, wod_hbm,
    latent_new, pairs_out, queries_out, bias_out, grid_v, wod_v,
    latent_v, ggain_v, ngain_v, dgain_v, wq_v, wkv_v, wo_v, wqd_v, wkvd_v, need_v, slot_v, count_v, dslot_v,
    table_v, normed, band_pairs, rows, query_mine, edges_mine,
    need_all, query_all, edges_all, latents_all, mix_send, stat_send, mix_all, stat_all, mixes_all, pairs_mine, pairs_in,
    node_of, worth_of, load_sem, send_sem, recv_sem, push_sem, pair_send, pair_recv,
):
    me = lax.axis_index("dom")
    nodes, model = latent_v.shape
    width = wq_v.shape[1]
    head = width // HEADS
    cap = need_v.shape[1] // peers
    group = 128 // cap
    chips = peers // 2
    side = lax.rem(me, 2)
    partner = me + 1 - 2 * side
    points = grid_v.shape[0]
    lanes = HEADS * nodes
    both = 2 * cap
    quad = 4
    here = me // 2
    beside = here + 1 - 2 * lax.rem(here, 2)
    blocks = BLOCKS
    block = points // blocks

    barrier = pltpu.get_barrier_semaphore()
    for to in [lax.rem(me + 2 * step, peers) for step in range(1, chips)] + [partner]:
        pl.semaphore_signal(barrier, inc=1, device_id={"dom": to}, device_id_type=pl.DeviceIdType.MESH)

    def block_at(number):
        return slice(number * block, (number + 1) * block)

    pairs_of_refs = {
        "slot": (slot_hbm, slot_v), "count": (count_hbm, count_v), "need": (need_hbm, need_v),
        "latent": (latent_hbm, latent_v), "ngain": (ngain_hbm, ngain_v), "wq": (wq_hbm, wq_v),
        "ggain": (ggain_hbm, ggain_v),
    }
    for number in range(blocks):
        pairs_of_refs[number] = (grid_hbm.at[block_at(number)], grid_v.at[block_at(number)])
    pairs_of_refs.update({
        "wkv": (wkv_hbm, wkv_v), "wqd": (wqd_hbm, wqd_v), "dslot": (dslot_hbm, dslot_v), "table": (table_hbm, table_v),
        "wo": (wo_hbm, wo_v), "dgain": (dgain_hbm, dgain_v), "wkvd": (wkvd_hbm, wkvd_v), "wod": (wod_hbm, wod_v),
    })
    loads = {}
    for number, (name, (source, target)) in enumerate(pairs_of_refs.items()):
        loads[name] = pltpu.make_async_copy(source, target, load_sem.at[number])
        loads[name].start()

    def message(kind, source, target, to, landing=None):
        return pltpu.make_async_remote_copy(
            src_ref=source,
            dst_ref=target,
            send_sem=send_sem.at[kind],
            recv_sem=recv_sem.at[kind if landing is None else landing],
            device_id={"dom": to},
            device_id_type=pl.DeviceIdType.MESH,
        )

    def chip(step):
        return lax.rem(me + 2 * step, peers)

    def place(step):
        return lax.rem(here + step, chips)

    def exchange(kind, buffer):
        rest = buffer.at[pl.ds(1, chips - 1)]
        return message(kind, rest, rest, partner)

    def need_to(step):
        return message(0, need_v, need_all.at[chips - step], chip(step))

    def edges_to(step):
        return message(1, edges_mine.at[place(step)], edges_all.at[chips - step], chip(step))

    def query_to(step):
        return message(2, query_mine, query_all.at[chips - step], chip(step))

    def mix_to(step):
        return message(3, mix_send.at[step], mix_all.at[chips - step], chip(step))

    def stat_to(step):
        return message(4, stat_send.at[step], stat_all.at[chips - step], chip(step))

    def mixes_to(step):
        return message(5, mixes_all.at[0], mixes_all.at[chips - step], chip(step))

    apart = chips + here - beside

    def latent_to(step, slot):
        return message(6, latents_all.at[0], latents_all.at[slot], chip(step), 6 + slot // 2)

    def latent_from(slot):
        return message(6, latents_all.at[slot], latents_all.at[slot], partner, 6 + slot // 2)

    def latent_on(slot):
        return message(
            6, latents_all.at[slot], latents_all.at[lax.rem(slot + apart, chips)], 2 * beside + side, 6
        )

    def latents_beside():
        some = latents_all.at[pl.ds(0, chips // 2)]
        return message(6, some, some, partner, 6)

    push_whole = pltpu.make_async_remote_copy(
        src_ref=band_pairs.at[0],
        dst_ref=band_pairs.at[1],
        send_sem=push_sem.at[0],
        recv_sem=push_sem.at[1],
        device_id={"dom": partner},
        device_id_type=pl.DeviceIdType.MESH,
    )

    def pair_over(number):
        return pltpu.make_async_remote_copy(
            src_ref=pairs_mine.at[number],
            dst_ref=pairs_in.at[number],
            send_sem=pair_send.at[number],
            recv_sem=pair_recv.at[number],
            device_id={"dom": partner},
            device_id_type=pl.DeviceIdType.MESH,
        )

    def push(number):
        return pltpu.make_async_remote_copy(
            src_ref=band_pairs.at[0, block_at(number)],
            dst_ref=band_pairs.at[1, block_at(number)],
            send_sem=push_sem.at[0],
            recv_sem=push_sem.at[1],
            device_id={"dom": partner},
            device_id_type=pl.DeviceIdType.MESH,
        )

    others = [step for low in range(1, chips // 2) for step in (low, chips - low)] + [chips // 2]
    alike = range(2, chips, 2)

    loads["slot"].wait()
    loads["count"].wait()
    edge_total = slot_v.shape[1]
    own = iota((nodes, nodes), 0) == iota((nodes, nodes), 1)
    counts = jnp.sum(jnp.where(own, count_v[...].astype(F32), 0.0), axis=1, keepdims=True)
    slots = jnp.where(iota(slot_v.shape, 1).astype(F32) < counts, slot_v[...], -1)
    entry = iota((nodes, peers * cap), 1)
    tally = jnp.zeros((nodes, peers * cap), F32)
    for j in range(edge_total):
        tally = tally + jnp.where(slots[:, j : j + 1] == entry, 1.0, 0.0)
    tally = tally.astype(BF16)
    for number in range(chips):
        own_part = tally[:, number * both : (number + 1) * both]
        edges_mine[number] = jnp.concatenate([own_part] * (128 // both), axis=1)
    edges_all[0] = edges_mine[here]
    loads["need"].wait()
    need_all[0] = need_v[...]
    loads["latent"].wait()
    loads["ngain"].wait()
    loads["wq"].wait()
    queries = jnp.dot(
        norm_into(latent_v[...], ngain_v[...]), wq_v[...], preferred_element_type=F32
    ).astype(BF16)
    query_mine[...] = queries
    query_all[0] = queries
    latents_all[0] = latent_v[...]

    pl.semaphore_wait(barrier, chips)
    for step in others:
        need_to(step).start()
    for step in others:
        edges_to(step).start()
        query_to(step).start()

    loads["ggain"].wait()
    for number in range(blocks):
        loads[number].wait()
    loads["wkv"].wait()
    settled = norm_into(grid_v[block_at(0), :], ggain_v[...])
    for number in range(blocks):
        at = block_at(number)
        normed[at, :] = settled
        band_pairs[0, at, :] = jnp.dot(settled, wkv_v[...], preferred_element_type=F32).astype(BF16)
        if number + 1 < blocks:
            settled = norm_into(grid_v[block_at(number + 1), :], ggain_v[...])
        push(number).start()
    for step in alike:
        latent_to(step, chips - step).start()
    latent_on(0).start()

    exchange(0, need_all).wait_recv()
    base = pl.multiple_of((me // group) * 128, 128)
    lists = need_all[:, :, pl.ds(base, 128)]
    within = lax.rem(me // 2, group // 2) * both
    asked = jnp.broadcast_to(lists, (chips, cap, 128)).astype(F32)
    spot = iota((chips, cap, 128), 1)
    lane = iota((chips, cap, 128), 2)
    wanted = []
    for band in (side, 1 - side):
        picked = jnp.where(lane == within + band * cap + spot, asked, 0.0)
        wanted.append(jnp.sum(picked, axis=2, keepdims=True).astype(jnp.int32).reshape(chips * cap, 1))
    point = iota((chips * cap, points), 1)
    def pick_of(band):
        return jnp.where(wanted[band] == point, 1.0, 0.0).astype(BF16)

    def rows_of(band, part):
        lane = slice(part * width, (part + 1) * width)
        return jnp.dot(pick_of(band), band_pairs[band, :, lane], preferred_element_type=F32).astype(BF16)

    for part in range(2):
        rows[part, side] = rows_of(0, part)
    exchange(1, edges_all).wait_recv()
    exchange(2, query_all).wait_recv()
    push_whole.wait_recv()
    rows[0, 1 - side] = rows_of(1, 0)

    scale = math.log2(math.e) / math.sqrt(head)
    span = quad * head
    own_head = iota((quad * nodes, span), 0) // nodes == iota((quad * nodes, span), 1) // head
    tasks = [(step, four) for step in range(chips) for four in range(HEADS // quad)]

    def score(step, four):
        lane = slice(four * span, (four + 1) * span)
        at = slice(step * cap, (step + 1) * cap)
        query = jnp.concatenate([query_all[step][:, lane]] * quad, axis=0)
        query = jnp.where(own_head, query, jnp.zeros_like(query))
        keys_here = jnp.concatenate([rows[0, 0, at, lane], rows[0, 1, at, lane]], axis=0)
        return lax.dot_general(query, keys_here, NT, preferred_element_type=F32)

    def soften(step, scores):
        times = jnp.concatenate([edges_all[step][:, :both].astype(F32)] * quad, axis=0)
        scores = jnp.where(times > 0, scores * scale, -1e30)
        highest = jnp.max(scores, axis=1, keepdims=True)
        raised = jnp.exp2(scores - highest) * times
        return raised.astype(BF16), jnp.broadcast_to(highest, (quad * nodes, 128))

    def blend(step, four, raised):
        lane = slice(four * span, (four + 1) * span)
        at = slice(step * cap, (step + 1) * cap)
        values_here = jnp.concatenate([rows[1, 0, at, lane], rows[1, 1, at, lane]], axis=0)
        mixed = jnp.dot(raised, values_here, preferred_element_type=F32)
        mixed = jnp.where(own_head, mixed, 0.0)
        return functools.reduce(jnp.add, [mixed[j * nodes : (j + 1) * nodes] for j in range(quad)]).astype(BF16)

    stat_lane = iota((lanes, 128), 1)
    board = jnp.zeros((lanes, 128), F32)
    every = jnp.ones((both, 128), BF16)
    scored = [score(step, four) for step, four in tasks]
    rows[1, 1 - side] = rows_of(1, 1)
    softened = [soften(step, one) for (step, four), one in zip(tasks, scored)]
    for (step, four), one in zip(tasks, softened):
        mixes = mix_all if step == 0 else mix_send
        mixes[step, :, four * span : (four + 1) * span] = blend(step, four, one[0])
    for step in range(chips):
        pair = softened[step * (HEADS // quad) : (step + 1) * (HEADS // quad)]
        totals = [jnp.dot(one[0], every, preferred_element_type=F32) for one in pair]
        board = jnp.where(stat_lane == step, jnp.concatenate([one[1] for one in pair], axis=0), board)
        board = jnp.where(stat_lane == chips + step, jnp.concatenate(totals, axis=0), board)
    board = board.T
    for step in range(chips):
        stats = stat_all if step == 0 else stat_send
        stats[step, 0:1, :] = board[step : step + 1]
        stats[step, 1:2, :] = board[chips + step : chips + step + 1]
    for step in others:
        stat_to(step).start()
        mix_to(step).start()

    for step in alike:
        latent_from(step).wait_recv()
        latent_on(step).start()

    loads["wqd"].wait()
    queries_out[...] = (jnp.dot(normed[...], wqd_v[...], preferred_element_type=F32) * scale).astype(BF16)

    loads["wo"].wait()
    loads["dgain"].wait()
    loads["wkvd"].wait()

    exchange(4, stat_all).wait_recv()
    tops = [stat_all[step, 0:1, :] for step in range(chips)]
    sums = [stat_all[step, 1:2, :] for step in range(chips)]
    top = functools.reduce(jnp.maximum, tops)
    shares = [jnp.exp2(one - top) for one in tops]
    whole = functools.reduce(jnp.add, [a * b for a, b in zip(shares, sums)])
    own_node = iota((nodes, lanes), 0) == lax.rem(iota((nodes, lanes), 1), nodes)
    stacked = jnp.concatenate([jnp.where(own_node, share / whole, 0.0) for share in shares], axis=0)
    widen = (iota((lanes, width), 0) // nodes == iota((lanes, width), 1) // head).astype(F32)
    factors = jnp.dot(stacked, widen, precision=HIGH, preferred_element_type=F32).reshape(chips, nodes, width)
    exchange(3, mix_all).wait_recv()
    enc_mixed = jnp.sum(factors * mix_all[...].astype(F32), axis=0).astype(BF16)
    mixes_all[0] = enc_mixed
    for step in others:
        mixes_to(step).start()

    loads["dslot"].wait()
    loads["table"].wait()
    keys = peers * nodes
    dec_cap = table_v.shape[0] * 128 // peers
    slots = dslot_v[...]
    edge_total = slots.shape[0]
    slots = jnp.concatenate([slots] * (8 // edge_total), axis=0)
    columns = []
    for part in range(points // 128):
        piece = slots[:, part * 128 : (part + 1) * 128]
        high = piece // 128
        low = lax.rem(piece, 128)
        need = jnp.zeros_like(piece)
        for line in range(table_v.shape[0]):
            entry = jnp.broadcast_to(table_v[line : line + 1, :], piece.shape)
            need = jnp.where(high == line, jnp.take_along_axis(entry, low, axis=1), need)
        owner = piece // dec_cap
        columns.append(lax.rem(owner, 2) * (chips * nodes) + lax.rem(owner // 2 - here + chips, chips) * nodes + need)
    node = jnp.concatenate(columns, axis=1)
    times = jnp.ones(node.shape, F32)
    for j in range(1, edge_total):
        times = times + jnp.where(node == jnp.concatenate([node[j:], node[:j]], axis=0), 1.0, 0.0)
    node_of[...] = node.astype(F32).T
    worth_of[...] = jnp.log2(times).T
    name = iota((128, keys), 1).astype(F32)

    def bias_block(piece, carry):
        at = pl.ds(pl.multiple_of(piece * 128, 128), 128)
        nodes_here, worth_here = node_of[at, :], worth_of[at, :]
        bias = jnp.full((128, keys), -1e30, F32)
        for j in range(edge_total):
            bias = jnp.where(nodes_here[:, j : j + 1] == name, worth_here[:, j : j + 1], bias)
        bias_out[at, :] = bias
        return carry

    lax.fori_loop(0, points // 128, bias_block, 0)

    latents_beside().wait_recv()
    exchange(5, mixes_all).wait_recv()
    side_nodes = chips * nodes
    update = jnp.dot(mixes_all[...].reshape(side_nodes, width), wo_v[...], preferred_element_type=F32)
    fresh = (latents_all[...].reshape(side_nodes, model).astype(F32) + update).astype(BF16)
    settled = norm_into(fresh, dgain_v[...])
    for number in range(2):
        half = jnp.dot(settled, wkvd_v[:, number * width : (number + 1) * width], preferred_element_type=F32).astype(BF16)
        pairs_mine[number] = half
        pair_over(number).start()
    latent_new[...] = fresh[:nodes]
    near = pl.ds(pl.multiple_of(side * side_nodes, side_nodes), side_nodes)
    over = pl.ds(pl.multiple_of((1 - side) * side_nodes, side_nodes), side_nodes)
    for number in range(2):
        pairs_out[number, near, :] = pairs_mine[number]
    for kind, buffer in enumerate((need_all, edges_all, query_all, mix_all, stat_all, mixes_all, latents_all)):
        exchange(kind, buffer).wait_send()
    push_whole.wait_send()
    loads["wod"].wait()
    for number in range(2):
        pair_over(number).wait_recv()
        pairs_out[number, over, :] = pairs_in[number]

    for number in range(2):
        pair_over(number).wait_send()


BLOCKS = 4


VMEM_LIMIT = 32 * 1024 * 1024


def encode(grid, latent_in, grid_gain, node_gain, dec_gain, w_q_enc, w_kv_enc, w_o_enc, w_q_dec, w_kv_dec, w_o_dec,
           enc_need, enc_slot, enc_count, dec_slot, dec_need):
    peers = lax.axis_size("dom")
    nodes, model = latent_in.shape
    width = w_q_enc.shape[1]
    entries = enc_need.shape[1]
    cap = entries // peers
    points = grid.shape[0]
    chips = peers // 2
    lanes = HEADS * nodes
    far = pl.BlockSpec(memory_space=pltpu.HBM)
    vmem = pl.BlockSpec(memory_space=pltpu.VMEM)
    operands = (grid, latent_in, grid_gain[None], node_gain[None], dec_gain[None], w_q_enc, w_kv_enc, w_o_enc, w_q_dec,
                w_kv_dec, enc_need, enc_slot.T, enc_count[None], dec_slot, dec_need.reshape(-1, 128), w_o_dec)
    return pl.pallas_call(
        functools.partial(encoder_kernel, peers),
        name="encode",
        out_shape=(
            pltpu.VMEM((nodes, model), BF16),
            pltpu.VMEM((2, peers * nodes, width), BF16),
            pltpu.VMEM((points, width), BF16),
            pltpu.VMEM((points, peers * nodes), F32),
            pltpu.VMEM(grid.shape, BF16),
            pltpu.VMEM(w_o_dec.shape, BF16),
        ),
        in_specs=[far] * len(operands),
        out_specs=(vmem,) * 6,
        scratch_shapes=[pltpu.VMEM(one.shape, one.dtype) for one in operands[1:-1]] + [
            pltpu.VMEM((points, model), BF16),
            pltpu.VMEM((2, points, 2 * width), BF16),
            pltpu.VMEM((2, 2, chips * cap, width), BF16),
            pltpu.VMEM((nodes, width), BF16),
            pltpu.VMEM((chips, nodes, 128), BF16),
            pltpu.VMEM((chips, 1, entries), jnp.int32),
            pltpu.VMEM((chips, nodes, width), BF16),
            pltpu.VMEM((chips, nodes, 128), BF16),
            pltpu.VMEM((chips, nodes, model), BF16),
            pltpu.VMEM((chips, nodes, width), BF16),
            pltpu.VMEM((chips, 2, lanes), F32),
            pltpu.VMEM((chips, nodes, width), BF16),
            pltpu.VMEM((chips, 2, lanes), F32),
            pltpu.VMEM((chips, nodes, width), BF16),
            pltpu.VMEM((2, chips * nodes, width), BF16),
            pltpu.VMEM((2, chips * nodes, width), BF16),
            pltpu.VMEM((points, 8), F32),
            pltpu.VMEM((points, 8), F32),
            pltpu.SemaphoreType.DMA((len(operands) - 1 + BLOCKS,)),
            pltpu.SemaphoreType.DMA((7,)),
            pltpu.SemaphoreType.DMA((6 + chips // 2,)),
            pltpu.SemaphoreType.DMA((2,)),
            pltpu.SemaphoreType.DMA((2,)),
            pltpu.SemaphoreType.DMA((2,)),
        ],
        compiler_params=pltpu.CompilerParams(collective_id=0, has_side_effects=True, vmem_limit_bytes=VMEM_LIMIT),
    )(*[pltpu.with_memory_space_constraint(one, pltpu.HBM) for one in operands])


def decoder_kernel(latent_ref, pairs_v, query_v, bias_v, grid_v, wo_v, latent_hbm, out_hbm,
                   out_v, mixed, store_sem):
    points, width = query_v.shape
    head = width // HEADS
    keys = pairs_v.shape[1]
    quad = 4

    def rows(part, size):
        return slice(part * size, (part + 1) * size)

    stores = [pltpu.make_async_copy(latent_ref, latent_hbm, store_sem.at[PIECES])]
    stores[0].start()
    lane_head = iota((keys, quad * head), 1) // head
    side_of = iota((keys, 2 * head), 1) // head

    def keys_of(h):
        some = pairs_v[0, :, (h // quad) * quad * head : (h // quad + 1) * quad * head]
        return jnp.where(lane_head == h % quad, some, jnp.zeros_like(some))

    def values_of(pair):
        some = pairs_v[1, :, pair * 2 * head : (pair + 1) * 2 * head]
        none, one = jnp.zeros_like(some), jnp.ones_like(some)
        return jnp.concatenate([
            jnp.concatenate([jnp.where(side_of == side, some, none), jnp.where(side_of == side, one, none)], axis=1)
            for side in range(2)
        ], axis=0)

    def attend(pair, at):
        four = 2 * pair // quad
        query = query_v[at, four * quad * head : (four + 1) * quad * head]
        raised = []
        for side in range(2):
            scores = lax.dot_general(query, keys_of(2 * pair + side), NT, preferred_element_type=F32)
            scores = scores + bias_v[at, :]
            highest = jnp.max(scores, axis=1, keepdims=True)
            raised.append(jnp.exp2(scores - highest).astype(BF16))
        got = jnp.dot(jnp.concatenate(raised, axis=1), values_of(pair), preferred_element_type=F32)
        mixed[at, pair * 2 * head : (pair + 1) * 2 * head] = (got[:, : 2 * head] / got[:, 2 * head :]).astype(BF16)

    def project(number, size):
        at = slice(number * size, (number + 1) * size)
        update = jnp.dot(mixed[at, :], wo_v[...], preferred_element_type=F32)
        out_v[at, :] = (grid_v[at, :].astype(F32) + update).astype(BF16)

    def leave(number, size):
        at = slice(number * size, (number + 1) * size)
        stores.append(pltpu.make_async_copy(out_v.at[at], out_hbm.at[at], store_sem.at[number]))
        stores[-1].start()

    for pair in range(HEADS // 2):
        for part in range(2):
            attend(pair, rows(part, points // 2))
    for number in range(PIECES):
        project(number, points // PIECES)
        leave(number, points // PIECES)
    for store in stores:
        store.wait()


PIECES = 8


def decode(latent_out, pairs, queries, bias, grid, w_o_dec):
    points, model = grid.shape
    width = queries.shape[1]
    vmem = pl.BlockSpec(memory_space=pltpu.VMEM)
    far = pl.BlockSpec(memory_space=pltpu.HBM)
    return pl.pallas_call(
        decoder_kernel,
        name="decode",
        out_shape=(
            jax.ShapeDtypeStruct(latent_out.shape, BF16),
            jax.ShapeDtypeStruct(grid.shape, BF16),
        ),
        in_specs=[vmem] * 6,
        out_specs=(far, far),
        scratch_shapes=[
            pltpu.VMEM(grid.shape, BF16),
            pltpu.VMEM((points, width), BF16),
            pltpu.SemaphoreType.DMA((PIECES + 1,)),
        ],
        compiler_params=pltpu.CompilerParams(vmem_limit_bytes=VMEM_LIMIT),
    )(latent_out, pairs, queries, bias, grid, w_o_dec)


def by_kernels(grid, latent_in, grid_gain, node_gain, dec_gain, w_q_enc, w_kv_enc, w_o_enc,
               w_q_dec, w_kv_dec, w_o_dec, enc_need, enc_slot, enc_count, dec_need, dec_slot):
    return decode(*encode(
        grid, latent_in, grid_gain, node_gain, dec_gain, w_q_enc, w_kv_enc, w_o_enc, w_q_dec, w_kv_dec, w_o_dec,
        enc_need, enc_slot, enc_count, dec_slot, dec_need))


def chosen_form(*args):
    grid, latent_in, enc_need, dec_slot = args[0], args[1], args[11], args[15]
    peers = lax.axis_size("dom")
    cap = enc_need.shape[1] // peers
    small = latent_in.shape[0] * peers <= 256
    fits = peers % 4 == 0 and 128 % cap == 0 and cap in (32, 64) and peers <= 128 and HEADS * latent_in.shape[0] == 128 and grid.shape[0] % 512 == 0
    if small and fits and 8 % dec_slot.shape[0] == 0:
        return by_kernels(*args)
    return on_device(*args)


def solution(mesh):
    both, rep = P(("groups", "dom"), None), P()
    return jax.shard_map(
        chosen_form,
        mesh=mesh,
        in_specs=(both, both, *([rep] * 9), P("dom", None), P(None, "dom"), P("dom"), P("dom", None), P(None, "dom")),
        out_specs=(both, both),
        check_vma=False,
    )
```
